128 devices in a mesh: seq: 16 (over x, z), nbr: 4 (over y), batch: 2 (over core).
Axes of the slice: x: 4, y: 4, z: 4, core: 2. Of those that a mesh axis runs over, the one named last changes fastest.
Arguments:
- hidden: bfloat16 [4096, 4096], P(('batch', 'seq'), 'nbr'), parts along dimension 0, may hold values from -6 to 6
- d_out: bfloat16 [4096, 4096], P(('batch', 'seq'), 'nbr'), parts along dimension 0, may hold values from -6 to 6
- nbr_emb: bfloat16 [768, 128, 896], P(('batch', 'seq', 'nbr')), parts along dimension 0, may hold values from -6 to 6
- slot_span: int32 [768], P(('batch', 'seq')), parts along dimension 0, may hold values from -1 to 1, as said below
- dec_gain: bfloat16 [4096], P('nbr'), may hold values from 0.5 to 1.5
- enc_gain: bfloat16 [896], replicated, may hold values from 0.5 to 1.5
- w_cond: bfloat16 [4096, 896], P('nbr'), may hold values from -0.75 to 0.75
- w_enc: bfloat16 [896, 896], replicated, may hold values from -0.1875 to 0.1875
- w_q: bfloat16 [4096, 2048], P('seq', 'nbr'), may hold values from -0.09375 to 0.09375
- w_k: bfloat16 [896, 2048], P('seq', 'nbr'), may hold values from -8 to 8
- w_v: bfloat16 [896, 2048], P('seq', 'nbr'), may hold values from -0.1875 to 0.1875
- w_o: bfloat16 [2048, 4096], P('nbr', 'seq'), may hold values from -0.125 to 0.125
Outputs:
- out: bfloat16 [4096, 4096], P(('batch', 'seq'), 'nbr'), parts along dimension 0
- d_hidden: bfloat16 [4096, 4096], P(('batch', 'seq'), 'nbr'), parts along dimension 0
- d_enc: bfloat16 [768, 128, 896], P(('batch', 'seq', 'nbr')), parts along dimension 0
- d_wo: float32 [4096, 4096], P(('batch', 'nbr'), 'seq'), parts along dimension 0
- d_wk: float32 [1792, 2048], P(('batch', 'seq'), 'nbr'), parts along dimension 0
- d_wv: float32 [1792, 2048], P(('batch', 'seq'), 'nbr'), parts along dimension 0
The draws below stay inside these ranges and needn't reach their ends.
There are 2 independent parts, one for each index of `batch`. The reference program is written for one: setup_inputs(seed, part) draws one part's arguments, and reference() takes and returns one part's arrays. A program takes and returns all parts, laid end to end along the dimension named above; an argument that names none is the same for every part. Nothing has to cross between parts.
Inputs may be any that keep to these rules, and one draw needn't show every extreme that they name: `slot_span`: A slot on seq index s serves a span of seq index s, counted from 0 within its 2 spans; -1 marks an empty slot. Every span is served by 1 to 8 slots, and one span of each seq index by exactly 8. Within each seq index one nbr index has all 6 slots live.
All inputs are finite; a program needn't handle non-finite values.
Results may differ from the reference program's by a relative error of at most 0.018.
The reference program's roundings to bfloat16 on the way count: a program that leaves them out, or rounds other values in their place, can miss the bound.
Values may be sent and summed in bfloat16 or wider, within the bound.
No kernel may reach another device: no remote copies, remote signals or barrier semaphores. Data moves between devices by JAX's collectives and lax.ppermute only.
A program may use at most 128 MiB of HBM per device.

```python
import jax
import jax.numpy as jnp
from jax import lax

D = 4096
EW = 896
H = 16
HD = 128
CLEN = 64
NLEN = 128
KMAX = 8
NEIGHBOUR_SLOTS = 6
TOK_DEV = 128
TOKENS = 2048
SPANS_PER_INDEX = 2
SPANS = 32
GSLOT = 24
SLOTS = 384
HW = 2048
N_SEQ = 16
N_NBR = 4


def draw_group_index(group_random_key):
    slot_count = NEIGHBOUR_SLOTS * N_NBR
    batch_random_key, occupy_random_key, order_random_key, first_random_key = jax.random.split(group_random_key, 4)
    draw_batch = jax.random.randint(batch_random_key, (), 0, SPANS_PER_INDEX)
    span_index = jnp.arange(slot_count, dtype=jnp.int32)
    remaining_slots = span_index - SPANS_PER_INDEX - KMAX + 1
    other_device = (draw_batch + 1 + remaining_slots % (SPANS_PER_INDEX - 1)) % SPANS_PER_INDEX
    occupied_slots = (jax.random.randint(occupy_random_key, (slot_count,), 0, 4) == 0) & (remaining_slots < (KMAX - 1) * (SPANS_PER_INDEX - 1))
    group_label = jnp.where(span_index < SPANS_PER_INDEX, span_index, jnp.where(remaining_slots < 0, draw_batch, jnp.where(occupied_slots, other_device, -1)))
    group_label = group_label.astype(jnp.int32)
    shuffle = jax.random.permutation(order_random_key, slot_count).astype(jnp.int32)
    ranked = jnp.where(group_label >= 0, 0, slot_count) + shuffle
    order = jnp.argsort(ranked)
    ordered = group_label[order]
    first_slot = jax.random.randint(first_random_key, (), 0, N_NBR)
    device_index = (span_index // NEIGHBOUR_SLOTS + first_slot) % N_NBR
    target_device = (device_index * NEIGHBOUR_SLOTS + span_index % NEIGHBOUR_SLOTS).astype(jnp.int32)
    return jnp.zeros((slot_count,), jnp.int32).at[target_device].set(ordered)


def draw_slot_span(key, part):
    group_key_list = jax.random.split(jax.random.fold_in(key, 17), N_SEQ)
    return jax.vmap(draw_group_index)(group_key_list).reshape(N_SEQ * NEIGHBOUR_SLOTS * N_NBR)


def draw_w_k(key, part):
    k_base, k_heads = jax.random.split(jax.random.fold_in(key, 29))
    base = jnp.clip(jax.random.normal(k_base, (EW, HW), jnp.float32), -4.0, 4.0) * EW ** (-0.5)
    picked = jax.random.permutation(k_heads, H)
    column_head = jnp.arange(HW, dtype=jnp.int32) // HD
    strength = jnp.where(column_head == picked[0], 2.5, 1.0)
    return jnp.clip(base * strength[None, :].astype(jnp.float32), -8.0, 8.0).astype(jnp.bfloat16)


def steps_of(own_key, dims, cuts, least, high):
    def one(dim, parts):
        draws = jax.random.uniform(jax.random.fold_in(jax.random.fold_in(own_key, 6), dim), (parts,), jnp.float32, least / len(cuts), high / len(cuts))
        return jnp.repeat(jnp.exp(draws), dims[dim] // parts).reshape((-1,) + (1,) * (len(dims) - dim - 1))

    factor_of = one(*cuts[0])
    for cut in cuts[1:]:
        factor_of = factor_of * one(*cut)
    return factor_of


def bell_draw(rng, dims, scale, bound, shards=(), kind=jnp.bfloat16):
    result = jax.random.normal(rng, dims, jnp.float32) * scale
    if len(shards) > 0:
        result = steps_of(rng, dims, shards, -0.22, 0.18) * result
    return jnp.clip(result, min=-bound, max=bound).astype(kind)


def setup_inputs(seed: int = 0, part: int = 0) -> dict:
    key_list = jax.random.split(jax.random.key(seed), 13)
    part_splits = jax.random.split(jax.random.fold_in(key_list[12], part), 13)
    hidden = bell_draw(part_splits[0], (TOKENS, D), 1.0, 6.0, ((0, 16), (1, 4)))
    d_out = bell_draw(part_splits[1], (TOKENS, D), 1.0, 6.0, ((0, 16), (1, 4)))
    nbr_emb = bell_draw(part_splits[2], (SLOTS, NLEN, EW), 1.0, 6.0, ((0, 64),))
    slot_span = draw_slot_span(jax.random.fold_in(jax.random.fold_in(key_list[12], part), 71), part)
    dec_gain = jnp.clip(1.0 + 0.1 * jax.random.normal(key_list[4], (D,), jnp.float32), 0.5, 1.5).astype(jnp.bfloat16)
    enc_gain = jnp.clip(1.0 + 0.1 * jax.random.normal(key_list[5], (EW,), jnp.float32), 0.5, 1.5).astype(jnp.bfloat16)
    w_cond = bell_draw(key_list[6], (D, EW), (D // 64) ** -0.5, 0.75, ((0, 4),))
    w_enc = bell_draw(key_list[7], (EW, EW), EW ** -0.5, 0.1875)
    w_q = bell_draw(key_list[8], (D, HW), D ** -0.5, 0.09375, ((0, 16), (1, 4)))
    w_k = draw_w_k(jax.random.fold_in(key_list[12], 71), part)
    w_v = bell_draw(key_list[10], (EW, HW), EW ** -0.5, 0.1875, ((0, 16), (1, 4)))
    w_o = bell_draw(key_list[11], (HW, D), HW ** -0.5, 0.125, ((0, 4), (1, 16)))
    return dict(hidden=hidden, d_out=d_out, nbr_emb=nbr_emb, slot_span=slot_span, dec_gain=dec_gain, enc_gain=enc_gain, w_cond=w_cond, w_enc=w_enc, w_q=w_q, w_k=w_k, w_v=w_v, w_o=w_o)


def rms_scale(values):
    return lax.rsqrt(lax.optimization_barrier(jnp.mean(values * values, axis=-1, keepdims=True)) + 1e-06)

def group_attention(operands):
    query, keys, values, d_attn, owners = operands
    factor = HD ** (-0.5)
    token_span = jnp.arange(TOK_DEV, dtype=jnp.int32) // CLEN
    key_span = jnp.repeat(owners, NLEN)
    allowed = token_span[:, None] == key_span[None, :]
    qf = query.astype(jnp.float32)
    kf = keys.astype(jnp.float32)
    vf = values.astype(jnp.float32)
    df = d_attn.astype(jnp.float32)
    scores = jnp.einsum('thd,khd->htk', qf, kf) * factor
    scores = jnp.where(allowed[None], scores, -1e+30)
    peak = lax.optimization_barrier(jnp.max(scores, axis=-1, keepdims=True))
    weights = jnp.exp(scores - peak)
    probs = weights / lax.optimization_barrier(jnp.sum(weights, axis=-1, keepdims=True))
    probs_b = probs.astype(jnp.bfloat16)
    pf = probs_b.astype(jnp.float32)
    attended = jnp.einsum('htk,khd->thd', pf, vf).astype(jnp.bfloat16)
    d_probs = jnp.einsum('thd,khd->htk', df, vf)
    row_dot = lax.optimization_barrier(jnp.sum(probs * d_probs, axis=-1, keepdims=True))
    d_scores = (probs * (d_probs - row_dot) * factor).astype(jnp.bfloat16).astype(jnp.float32)
    d_query = jnp.einsum('htk,khd->thd', d_scores, kf).astype(jnp.bfloat16)
    d_key = jnp.einsum('htk,thd->khd', d_scores, qf).astype(jnp.bfloat16)
    d_value = jnp.einsum('htk,thd->khd', pf, df).astype(jnp.bfloat16)
    return (attended, d_query, d_key, d_value)

def reference(hidden, d_out, nbr_emb, slot_span, dec_gain, enc_gain, w_cond, w_enc, w_q, w_k, w_v, w_o):
    hf = hidden.astype(jnp.float32)
    pooled = lax.optimization_barrier(jnp.mean(hf.reshape(SPANS, CLEN, D), axis=1)).astype(jnp.bfloat16)
    before = jnp.concatenate([jnp.zeros((1, D), jnp.bfloat16), pooled[:SPANS - 1]], axis=0)
    cond = jnp.dot(before, w_cond, preferred_element_type=jnp.float32)
    group_index = jnp.arange(SLOTS, dtype=jnp.int32) // GSLOT
    live = slot_span >= 0
    served = (group_index * SPANS_PER_INDEX + jnp.maximum(slot_span, 0)).astype(jnp.int32)
    slot_cond = jnp.where(live[:, None], cond[served], jnp.float32(0.0))
    inputs = nbr_emb.astype(jnp.float32) + slot_cond[:, None, :]
    enc_normed = (inputs * rms_scale(inputs) * enc_gain.astype(jnp.float32)).astype(jnp.bfloat16)
    mixed = jnp.dot(enc_normed.reshape(-1, EW), w_enc, preferred_element_type=jnp.float32).reshape(inputs.shape)
    encoded = (inputs + jax.nn.silu(mixed)).astype(jnp.bfloat16)
    enc_rows = encoded.reshape(-1, EW)
    rstd = rms_scale(hf)
    normed = (hf * rstd * dec_gain.astype(jnp.float32)).astype(jnp.bfloat16)
    query = jnp.dot(normed, w_q, preferred_element_type=jnp.float32).astype(jnp.bfloat16)
    keys = jnp.dot(enc_rows, w_k, preferred_element_type=jnp.float32).astype(jnp.bfloat16)
    values = jnp.dot(enc_rows, w_v, preferred_element_type=jnp.float32).astype(jnp.bfloat16)
    d_attn = jnp.dot(d_out, w_o.T, preferred_element_type=jnp.float32).astype(jnp.bfloat16)
    attended, d_query, d_key, d_value = lax.map(group_attention, (query.reshape(N_SEQ, TOK_DEV, H, HD), keys.reshape(N_SEQ, GSLOT * NLEN, H, HD), values.reshape(N_SEQ, GSLOT * NLEN, H, HD), d_attn.reshape(N_SEQ, TOK_DEV, H, HD), slot_span.reshape(N_SEQ, GSLOT)))
    attended = attended.reshape(TOKENS, HW)
    d_query = d_query.reshape(TOKENS, HW)
    d_key = d_key.reshape(SLOTS * NLEN, HW)
    d_value = d_value.reshape(SLOTS * NLEN, HW)
    out = (hf + jnp.dot(attended, w_o, preferred_element_type=jnp.float32)).astype(jnp.bfloat16)
    d_wo = jnp.dot(attended.T, d_out, preferred_element_type=jnp.float32)
    d_wk = jnp.dot(enc_rows.T, d_key, preferred_element_type=jnp.float32)
    d_wv = jnp.dot(enc_rows.T, d_value, preferred_element_type=jnp.float32)
    block = HW // N_NBR
    total = jnp.zeros((SLOTS * NLEN, EW), jnp.float32)
    for span_index in range(N_NBR):
        lower = span_index * block
        upper = lower + block
        part = jnp.dot(d_key[:, lower:upper], w_k[:, lower:upper].T, preferred_element_type=jnp.float32)
        part = part + jnp.dot(d_value[:, lower:upper], w_v[:, lower:upper].T, preferred_element_type=jnp.float32)
        total = total + part.astype(jnp.bfloat16).astype(jnp.float32)
    d_enc = total.reshape(SLOTS, NLEN, EW).astype(jnp.bfloat16)
    d_normed = jnp.dot(d_query, w_q.T, preferred_element_type=jnp.float32)
    scaled_grad = dec_gain.astype(jnp.float32) * d_normed
    stat = lax.optimization_barrier(jnp.mean(hf * scaled_grad, axis=-1, keepdims=True))
    d_hidden = (d_out.astype(jnp.float32) + rstd * scaled_grad - hf * rstd ** 3 * stat).astype(jnp.bfloat16)
    return (out, d_hidden, d_enc, d_wo, d_wk, d_wv)
```

```python
import functools

import jax
import jax.numpy as jnp
from jax import lax
from jax.experimental import pallas as pl
from jax.experimental.pallas import tpu as pltpu
from jax.sharding import PartitionSpec as P

HD = 128
CLEN = 64
NLEN = 128
KMAX = 8
F32 = jnp.float32
BF16 = jnp.bfloat16
VMEM = pl.BlockSpec(memory_space=pltpu.VMEM)
SMEM = pl.BlockSpec(memory_space=pltpu.SMEM)


def dot(a, b, dims=((1,), (0,))):
    return lax.dot_general(a, b, (dims, ((), ())), preferred_element_type=F32)


NT = ((1,), (1,))
TN = ((0,), (0,))


def shift(x, by):
    n = lax.axis_size("nbr")
    return lax.ppermute(x, "nbr", [(i, (i + by) % n) for i in range(n)])


def ring_gather(x):
    half = x.shape[0] // 2
    right = shift(x, -1)
    left = shift(x, 1)
    far_a = shift(right[:half], -1)
    far_b = shift(left[half:], 1)
    return x, right, (far_a, far_b), left


def ring_scatter(parts):
    own, to_right, to_far, to_left = parts
    half = own.shape[0] // 2
    via_left = shift(to_far[:half], 1)
    via_right = shift(to_far[half:], -1)
    plain_left = shift(to_right[half:], 1)
    plain_right = shift(to_left[:half], -1)
    sum_right = (to_right[:half].astype(F32) + via_left.astype(F32)).astype(BF16)
    sum_left = (to_left[half:].astype(F32) + via_right.astype(F32)).astype(BF16)
    summed_left = shift(sum_right, 1)
    summed_right = shift(sum_left, -1)
    low = own[:half].astype(F32) + summed_left.astype(F32) + plain_right.astype(F32)
    high = own[half:].astype(F32) + plain_left.astype(F32) + summed_right.astype(F32)
    return low, high


def sum_small(x):
    return x + shift(x, 1) + shift(x, 2) + shift(x, 3)


def rms_scale(values):
    return lax.rsqrt(jnp.mean(values * values, axis=-1, keepdims=True) + 1e-06)


def project_kernel(n_ref, x_ref, d_ref, w_ref, q_ref, dc_ref, qa, da):
    step = pl.program_id(0)
    x, d, w = x_ref[0], d_ref[0], w_ref
    q = jnp.zeros(qa.shape, F32)
    dc = jnp.zeros(da.shape, F32)
    for s in range(4):
        wq = w[2 * s : 2 * s + 2, 0:128, :].reshape(256, 512)
        wo = w[2 * s : 2 * s + 2, 128:256, :].reshape(256, 512)
        q += dot(x[:, 256 * s : 256 * s + 256], wq)
        dc += dot(d[:, 256 * s : 256 * s + 256], wo)

    @pl.when(step == 0)
    def _():
        qa[...] = q
        da[...] = dc

    @pl.when(step > 0)
    def _():
        qa[...] += q
        da[...] += dc

    @pl.when(step == 3)
    def _():
        q_ref[...] = qa[...].astype(BF16)
        dc_ref[...] = da[...].astype(BF16)


def project(n, normed, dout, weights):
    tokens = normed.shape[1]
    return pl.pallas_call(
        project_kernel,
        grid_spec=pltpu.PrefetchScalarGridSpec(
            num_scalar_prefetch=1,
            grid=(4,),
            in_specs=[
                pl.BlockSpec((1, tokens, 1024), lambda r, n: (r, 0, 0)),
                pl.BlockSpec((1, tokens, 1024), lambda r, n: (r, 0, 0)),
                pl.BlockSpec((8, 256, 512), lambda r, n: ((n[0] + r) % 4, 0, 0)),
            ],
            out_specs=[
                pl.BlockSpec((tokens, 512), lambda r, n: (0, 0)),
                pl.BlockSpec((tokens, 512), lambda r, n: (0, 0)),
            ],
            scratch_shapes=[pltpu.VMEM((tokens, 512), F32)] * 2,
        ),
        out_shape=[jax.ShapeDtypeStruct((tokens, 512), BF16)] * 2,
        compiler_params=pltpu.CompilerParams(vmem_limit_bytes=32 << 20),
        name="project",
    )(n, normed, dout, weights)


def attend_kernel(tab, e0, e1, e2a, e2b, e3, wk, wv, q, dc, enc, ctx, dq, dk, dv, kb, vb):
    half = e2a.shape[0]
    tables = ((e0, 0), (e1, 6), (e2a, 12), (e2b, 12 + half), (e3, 18))

    def pick(j, carry):
        src = tab[j]

        @pl.when(src < 0)
        def _():
            enc[j] = jnp.zeros(enc.shape[1:], BF16)

        for ref, first in tables:

            @pl.when((src >= first) & (src < first + ref.shape[0]))
            def _(ref=ref, first=first):
                enc[j] = ref[src - first]

        return carry

    lax.fori_loop(0, 2 * KMAX, pick, 0)

    def kv(c, carry):
        x = enc[pl.ds(4 * c, 4)].reshape(4 * NLEN, enc.shape[2])
        rows = pl.ds(pl.multiple_of(c * 512, 512), 512)
        kb[rows, :] = dot(x, wk[...]).astype(BF16)
        vb[rows, :] = dot(x, wv[...]).astype(BF16)
        return carry

    lax.fori_loop(0, 4, kv, 0)
    factor = HD ** (-0.5)
    heads = q.shape[1] // HD
    keys = KMAX * NLEN
    for c in range(2):
        limit = tab[2 * KMAX + c] * NLEN
        allowed = lax.broadcasted_iota(jnp.int32, (CLEN, keys), 1) < limit
        toks = slice(c * CLEN, (c + 1) * CLEN)
        rows = slice(c * keys, (c + 1) * keys)
        for h in range(heads):
            cols = slice(h * HD, (h + 1) * HD)
            qh, dh = q[toks, cols], dc[toks, cols]
            kh, vh = kb[rows, cols], vb[rows, cols]
            s = jnp.where(allowed, dot(qh, kh, NT) * factor, -1e30)
            w = jnp.exp(s - jnp.max(s, axis=-1, keepdims=True))
            p = w / jnp.sum(w, axis=-1, keepdims=True)
            pb = p.astype(BF16)
            ctx[toks, cols] = dot(pb, vh).astype(BF16)
            dp = dot(dh, vh, NT)
            rd = jnp.sum(p * dp, axis=-1, keepdims=True)
            ds = (p * (dp - rd) * factor).astype(BF16)
            dq[toks, cols] = dot(ds, kh).astype(BF16)
            dk[rows, cols] = dot(ds, qh, TN).astype(BF16)
            dv[rows, cols] = dot(pb, dh, TN).astype(BF16)


def attend(tab, blocks, wk, wv, q, dc):
    width = wk.shape[0]
    rows = 2 * KMAX * NLEN
    flat = jax.ShapeDtypeStruct((rows, q.shape[1]), BF16)
    same = jax.ShapeDtypeStruct(q.shape, BF16)
    return pl.pallas_call(
        attend_kernel,
        in_specs=[SMEM] + [VMEM] * 9,
        out_specs=[VMEM] * 5,
        out_shape=[jax.ShapeDtypeStruct((2 * KMAX, NLEN, width), BF16), same, same, flat, flat],
        scratch_shapes=[pltpu.VMEM((rows, q.shape[1]), BF16)] * 2,
        compiler_params=pltpu.CompilerParams(vmem_limit_bytes=48 << 20),
        name="attend",
    )(tab, *blocks, wk, wv, q, dc)


def spread_kernel(inv, dk, dv, wk, wv, o0, o1, o2, o3, de):
    def grad(c, carry):
        rows = pl.ds(pl.multiple_of(c * 512, 512), 512)
        part = dot(dk[rows, :], wk[...], NT) + dot(dv[rows, :], wv[...], NT)
        de[pl.ds(4 * c, 4)] = part.astype(BF16).reshape(4, NLEN, wk.shape[0])
        return carry

    lax.fori_loop(0, 4, grad, 0)

    def place(i, carry):
        for r, out in enumerate((o0, o1, o2, o3)):
            src = inv[r * 6 + i]

            @pl.when(src < 0)
            def _(out=out):
                out[i] = jnp.zeros(out.shape[1:], BF16)

            @pl.when(src >= 0)
            def _(out=out, src=src):
                out[i] = de[src]

        return carry

    lax.fori_loop(0, 6, place, 0)


def spread(inv, dk, dv, wk, wv):
    width = wk.shape[0]
    return pl.pallas_call(
        spread_kernel,
        in_specs=[SMEM] + [VMEM] * 4,
        out_specs=[VMEM] * 4,
        out_shape=[jax.ShapeDtypeStruct((6, NLEN, width), BF16)] * 4,
        scratch_shapes=[pltpu.VMEM((2 * KMAX, NLEN, width), BF16)],
        compiler_params=pltpu.CompilerParams(vmem_limit_bytes=48 << 20),
        name="spread",
    )(inv, dk, dv, wk, wv)


def unproject_kernel(n_ref, ctx, dq, w, o):
    for s in range(4):
        wq = w[2 * s : 2 * s + 2, 0:128, :].reshape(256, 512)
        wo = w[2 * s : 2 * s + 2, 128:256, :].reshape(256, 512)
        o[0, 0, :, 256 * s : 256 * s + 256] = dot(ctx[...], wo, NT).astype(BF16)
        o[0, 1, :, 256 * s : 256 * s + 256] = dot(dq[...], wq, NT).astype(BF16)


def unproject(n, ctx, dq, weights):
    tokens = ctx.shape[0]
    return pl.pallas_call(
        unproject_kernel,
        grid_spec=pltpu.PrefetchScalarGridSpec(
            num_scalar_prefetch=1,
            grid=(4,),
            in_specs=[
                pl.BlockSpec((tokens, 512), lambda r, n: (0, 0)),
                pl.BlockSpec((tokens, 512), lambda r, n: (0, 0)),
                pl.BlockSpec((8, 256, 512), lambda r, n: ((n[0] + r) % 4, 0, 0)),
            ],
            out_specs=pl.BlockSpec((1, 2, tokens, 1024), lambda r, n: (r, 0, 0, 0)),
        ),
        out_shape=jax.ShapeDtypeStruct((4, 2, tokens, 1024), BF16),
        compiler_params=pltpu.CompilerParams(vmem_limit_bytes=32 << 20),
        name="unproject",
    )(n, ctx, dq, weights)


def outer_kernel(n_ref, d, ctx, o):
    for s in range(4):
        o[s] = dot(d[0, :, 256 * s : 256 * s + 256], ctx[...], TN).astype(BF16)


def outer(n, dout, ctx):
    tokens = ctx.shape[0]
    return pl.pallas_call(
        outer_kernel,
        grid_spec=pltpu.PrefetchScalarGridSpec(
            num_scalar_prefetch=1,
            grid=(4,),
            in_specs=[
                pl.BlockSpec((1, tokens, 1024), lambda r, n: (r, 0, 0)),
                pl.BlockSpec((tokens, 512), lambda r, n: (0, 0)),
            ],
            out_specs=pl.BlockSpec((4, 256, 512), lambda r, n: ((n[0] + r) % 4, 0, 0)),
        ),
        out_shape=jax.ShapeDtypeStruct((16, 256, 512), BF16),
        compiler_params=pltpu.CompilerParams(vmem_limit_bytes=32 << 20),
        name="outer",
    )(n, dout, ctx)


def slot_tables(slot_span, n):
    rel = jnp.roll(slot_span.reshape(4, 6), -n, axis=0).reshape(-1)
    slots = rel.shape[0]
    ids = jnp.arange(slots, dtype=jnp.int32)
    before = ids[None, :] < ids[:, None]
    rank = jnp.sum((rel[None, :] == rel[:, None]) & before, axis=1, dtype=jnp.int32)
    where = jnp.where(rel >= 0, rel * KMAX + rank, -1).astype(jnp.int32)
    spot = jnp.arange(2 * KMAX, dtype=jnp.int32)
    hit = where[None, :] == spot[:, None]
    source = jnp.sum(jnp.where(hit, ids[None, :] + 1, 0), axis=1, dtype=jnp.int32) - 1
    counts = jnp.sum(rel[None, :] == jnp.arange(2)[:, None], axis=1, dtype=jnp.int32)
    return jnp.concatenate([source, counts]), where, rel


def body(hidden, d_out, nbr_emb, slot_span, dec_gain, enc_gain, w_cond, w_enc, w_q, w_k, w_v, w_o):
    n = lax.axis_index("nbr")
    b = lax.axis_index("batch")
    n1 = n.astype(jnp.int32).reshape(1)
    tokens, feats = hidden.shape
    spans = tokens // CLEN

    q_half = lax.dynamic_slice_in_dim(w_q, b * 128, 128, axis=0)
    o_half = lax.dynamic_slice_in_dim(w_o, b * 128, 128, axis=1).T
    kv_half = jnp.where(b == 0, w_k, w_v)
    weights = lax.all_gather(
        jnp.concatenate([q_half, o_half, kv_half], axis=0), ("seq", "batch"), axis=0
    )

    pooled = jnp.mean(hidden.astype(F32).reshape(spans, CLEN, feats), axis=1).astype(BF16)
    length = lax.axis_size("seq")
    carried = lax.ppermute(
        pooled[spans - 1 :], "seq", [(i, i + 1) for i in range(length - 1)]
    )
    previous = jnp.concatenate([carried, pooled[: spans - 1]], axis=0)
    condition = sum_small(jnp.dot(previous, w_cond, preferred_element_type=F32))

    e0, e1, (e2a, e2b), e3 = ring_gather(nbr_emb)
    gain_rows = jnp.broadcast_to(dec_gain[None], (8, feats))
    state = jnp.concatenate([hidden, gain_rows, d_out], axis=0)
    right, left = shift(state, -1), shift(state, 1)
    far_h, far_d = shift(right[: tokens + 8], -1), shift(left[tokens + 8 :], 1)

    tab, inv, rel_span = slot_tables(slot_span, n)

    def encode(block, first):
        own = lax.slice_in_dim(rel_span, first, first + block.shape[0])
        own = own[:, None, None]
        cond = jnp.where(own == 0, condition[0], jnp.where(own == 1, condition[1], 0.0))
        x = block.astype(F32) + cond
        enc_normed = (x * rms_scale(x) * enc_gain.astype(F32)).astype(BF16)
        width = x.shape[2]
        mixed = jnp.dot(
            enc_normed.reshape(-1, width), w_enc, preferred_element_type=F32
        ).reshape(x.shape)
        return (x + jax.nn.silu(mixed)).astype(BF16)

    encoded = [
        encode(e0, 0), encode(e1, 6), encode(e2a, 12), encode(e2b, 15), encode(e3, 18)
    ]

    hid_rel = jnp.stack([hidden, right[:tokens], far_h[:tokens], left[:tokens]])
    gain_rel = jnp.stack([dec_gain, right[tokens], far_h[tokens], left[tokens]])
    dout_rel = jnp.stack([d_out, right[tokens + 8 :], far_d, left[tokens + 8 :]])
    hf = hid_rel.astype(F32)
    rstd = lax.rsqrt(jnp.mean(hf * hf, axis=(0, 2)) + 1e-06)[:, None]
    normed = (hf * rstd[None] * gain_rel.astype(F32)[:, None, :]).astype(BF16)

    pairs = weights.reshape(16, 2, 312, 512)
    wk = pairs[:, 0, 256:].reshape(-1, 512)
    wv = pairs[:, 1, 256:].reshape(-1, 512)

    query, d_ctx = project(n1, normed, dout_rel, weights)
    enc, ctx, d_query, d_key, d_value = attend(tab, encoded, wk, wv, query, d_ctx)

    rows = enc.reshape(-1, enc.shape[2])
    d_wo_part = outer(n1, dout_rel, ctx)
    d_wk_part = dot(rows, d_key, TN).astype(BF16).reshape(16, -1, 512)
    d_wv_part = dot(rows, d_value, TN).astype(BF16).reshape(16, -1, 512)
    grads = jnp.concatenate([d_wo_part, d_wk_part, d_wv_part], axis=1)
    grads = lax.psum_scatter(grads, "seq", scatter_dimension=0, tiled=False).astype(F32)
    d_wo = grads[:256].T
    d_wk = grads[256:312]
    d_wv = grads[312:368]

    both = unproject(n1, ctx, d_query, weights)
    out_sum, own_grad = ring_scatter([both[0], both[1], both[2], both[3]])
    d_enc_low, d_enc_high = ring_scatter(spread(inv, d_key, d_value, wk, wv))
    d_enc = jnp.concatenate([d_enc_low, d_enc_high], axis=0).astype(BF16)

    own = hidden.astype(F32)
    out = (own + out_sum[0]).astype(BF16)
    scaled = dec_gain.astype(F32) * own_grad[0]
    stat = sum_small(jnp.sum(own * scaled, axis=-1, keepdims=True) / (4 * feats))
    d_hidden = d_out.astype(F32) + rstd * scaled - own * rstd**3 * stat
    return (out, d_hidden.astype(BF16), d_enc, d_wo, d_wk, d_wv)


def solution(mesh):
    placed = (
        P(("batch", "seq"), "nbr"),
        P(("batch", "seq"), "nbr"),
        P(("batch", "seq", "nbr"), None, None),
        P(("batch", "seq")),
        P("nbr"),
        P(),
        P("nbr", None),
        P(),
        P("seq", "nbr"),
        P("seq", "nbr"),
        P("seq", "nbr"),
        P("nbr", "seq"),
    )
    return jax.shard_map(
        body,
        mesh=mesh,
        in_specs=placed,
        out_specs=(
            P(("batch", "seq"), "nbr"),
            P(("batch", "seq"), "nbr"),
            P(("batch", "seq", "nbr"), None, None),
            P(("batch", "nbr"), "seq"),
            P(("batch", "seq"), "nbr"),
            P(("batch", "seq"), "nbr"),
        ),
        check_vma=False,
    )
```

```python
import jax
import jax.numpy as jnp
from jax import lax
from jax.experimental import pallas as pl
from jax.experimental.pallas import tpu as pltpu
from jax.sharding import PartitionSpec as P

HD = 128
CLEN = 64
NLEN = 128
KMAX = 8
F32 = jnp.float32
BF16 = jnp.bfloat16
VMEM = pl.BlockSpec(memory_space=pltpu.VMEM)
SMEM = pl.BlockSpec(memory_space=pltpu.SMEM)


def dot(a, b, dims=((1,), (0,))):
    return lax.dot_general(a, b, (dims, ((), ())), preferred_element_type=F32)


NT = ((1,), (1,))
TN = ((0,), (0,))


def shift(x, by):
    n = lax.axis_size("nbr")
    return lax.ppermute(x, "nbr", [(i, (i + by) % n) for i in range(n)])


def ring_gather(x):
    half = x.shape[0] // 2
    right = shift(x, -1)
    left = shift(x, 1)
    far_a = shift(right[:half], -1)
    far_b = shift(left[half:], 1)
    return right, far_a, far_b, left


def ring_scatter(own, to_right, to_far, to_left):
    half = own.shape[0] // 2
    via_left = shift(to_far[:half], 1)
    via_right = shift(to_far[half:], -1)
    plain_left = shift(to_right[half:], 1)
    plain_right = shift(to_left[:half], -1)
    sum_right = (to_right[:half].astype(F32) + via_left.astype(F32)).astype(BF16)
    sum_left = (to_left[half:].astype(F32) + via_right.astype(F32)).astype(BF16)
    summed_left = shift(sum_right, 1)
    summed_right = shift(sum_left, -1)
    low = own[:half].astype(F32) + summed_left.astype(F32) + plain_right.astype(F32)
    high = own[half:].astype(F32) + plain_left.astype(F32) + summed_right.astype(F32)
    return low, high


def ring_scatter_rows(parts):
    half = parts.shape[1] // 2
    via_left = shift(parts[2, :half], 1)
    via_right = shift(parts[2, half:], -1)
    low = jnp.arange(parts.shape[1])[:, None] < half
    far = jnp.concatenate([via_left, via_right], axis=0).astype(F32)
    to_right = (parts[1].astype(F32) + jnp.where(low, far, 0.0)).astype(BF16)
    to_left = (parts[3].astype(F32) + jnp.where(low, 0.0, far)).astype(BF16)
    from_left = shift(to_right, 1)
    from_right = shift(to_left, -1)
    return parts[0].astype(F32) + from_left.astype(F32) + from_right.astype(F32)


def sum_small(x):
    return x + shift(x, 1) + shift(x, 2) + shift(x, 3)


def rms_scale(values):
    return lax.rsqrt(jnp.mean(values * values, axis=-1, keepdims=True) + 1e-06)


def project_kernel(n_ref, x_ref, w, o_ref, acc):
    step = pl.program_id(0)
    x = x_ref[0]
    part = jnp.zeros(acc.shape, F32)
    for s in range(4):
        block = w[2 * s : 2 * s + 2].reshape(256, 512)
        part += dot(x[:, 256 * s : 256 * s + 256], block)

    @pl.when(step == 0)
    def _():
        acc[...] = part

    @pl.when((step > 0) & (step < 3))
    def _():
        acc[...] += part

    @pl.when(step == 3)
    def _():
        o_ref[...] = (acc[...] + part).astype(BF16)


def project(n, x, weights, row):
    tokens = x.shape[1]
    return pl.pallas_call(
        project_kernel,
        grid_spec=pltpu.PrefetchScalarGridSpec(
            num_scalar_prefetch=1,
            grid=(4,),
            in_specs=[
                pl.BlockSpec((1, tokens, 1024), lambda r, n: (r, 0, 0)),
                pl.BlockSpec((8, 128, 512), lambda r, n: ((n[0] + r) % 4, row, 0)),
            ],
            out_specs=pl.BlockSpec((tokens, 512), lambda r, n: (0, 0)),
            scratch_shapes=[pltpu.VMEM((tokens, 512), F32)],
        ),
        out_shape=jax.ShapeDtypeStruct((tokens, 512), BF16),
        compiler_params=pltpu.CompilerParams(vmem_limit_bytes=32 << 20),
        name="project",
    )(n, x, weights)


def forward_kernel(tab, e0, e1, e2a, e2b, e3, wk, wv, q, enc, ctx, probs, kb, vb):
    half = e2a.shape[0]
    tables = ((e0, 0), (e1, 6), (e2a, 12), (e2b, 12 + half), (e3, 18))

    def pick(j, carry):
        src = tab[j]

        @pl.when(src < 0)
        def _():
            enc[j] = jnp.zeros(enc.shape[1:], BF16)

        for ref, first in tables:

            @pl.when((src >= first) & (src < first + ref.shape[0]))
            def _(ref=ref, first=first):
                enc[j] = ref[src - first]

        return carry

    lax.fori_loop(0, 2 * KMAX, pick, 0)

    def kv(c, carry):
        x = enc[pl.ds(4 * c, 4)].reshape(4 * NLEN, enc.shape[2])
        rows = pl.ds(pl.multiple_of(c * 512, 512), 512)
        kb[rows, :] = dot(x, wk[...]).astype(BF16)
        vb[rows, :] = dot(x, wv[...]).astype(BF16)
        return carry

    lax.fori_loop(0, 4, kv, 0)
    factor = HD ** (-0.5)
    heads = q.shape[1] // HD
    keys = KMAX * NLEN
    for c in range(2):
        limit = tab[2 * KMAX + c] * NLEN
        allowed = lax.broadcasted_iota(jnp.int32, (CLEN, keys), 1) < limit
        toks = slice(c * CLEN, (c + 1) * CLEN)
        rows = slice(c * keys, (c + 1) * keys)
        for h in range(heads):
            cols = slice(h * HD, (h + 1) * HD)
            s = jnp.where(allowed, dot(q[toks, cols], kb[rows, cols], NT) * factor, -1e30)
            w = jnp.exp(s - jnp.max(s, axis=-1, keepdims=True))
            p = w / jnp.sum(w, axis=-1, keepdims=True)
            probs[c * heads + h] = p
            ctx[toks, cols] = dot(p.astype(BF16), vb[rows, cols]).astype(BF16)


def forward(tab, blocks, wk, wv, q):
    rows = 2 * KMAX * NLEN
    flat = jax.ShapeDtypeStruct((rows, q.shape[1]), BF16)
    probs = jax.ShapeDtypeStruct((2 * q.shape[1] // HD, CLEN, KMAX * NLEN), F32)
    return pl.pallas_call(
        forward_kernel,
        in_specs=[SMEM] + [VMEM] * 8,
        out_specs=[VMEM] * 5,
        out_shape=[
            jax.ShapeDtypeStruct((2 * KMAX, NLEN, wk.shape[0]), BF16),
            jax.ShapeDtypeStruct(q.shape, BF16),
            probs,
            flat,
            flat,
        ],
        compiler_params=pltpu.CompilerParams(vmem_limit_bytes=48 << 20),
        name="forward",
    )(tab, *blocks, wk, wv, q)


def backward_kernel(inv, probs, kb, vb, q, dc, wk, wv, dq, dk, dv, o0, o1, o2, o3, de):
    factor = HD ** (-0.5)
    heads = q.shape[1] // HD
    keys = KMAX * NLEN
    for c in range(2):
        toks = slice(c * CLEN, (c + 1) * CLEN)
        rows = slice(c * keys, (c + 1) * keys)
        for h in range(heads):
            cols = slice(h * HD, (h + 1) * HD)
            dh = dc[toks, cols]
            p = probs[c * heads + h]
            dp = dot(dh, vb[rows, cols], NT)
            rd = jnp.sum(p * dp, axis=-1, keepdims=True)
            ds = (p * (dp - rd) * factor).astype(BF16)
            dq[toks, cols] = dot(ds, kb[rows, cols]).astype(BF16)
            dk[rows, cols] = dot(ds, q[toks, cols], TN).astype(BF16)
            dv[rows, cols] = dot(p.astype(BF16), dh, TN).astype(BF16)

    def grad(c, carry):
        rows = pl.ds(pl.multiple_of(c * 512, 512), 512)
        part = dot(dk[rows, :], wk[...], NT) + dot(dv[rows, :], wv[...], NT)
        de[pl.ds(4 * c, 4)] = part.astype(BF16).reshape(4, NLEN, wk.shape[0])
        return carry

    lax.fori_loop(0, 4, grad, 0)

    def place(i, carry):
        for r, out in enumerate((o0, o1, o2, o3)):
            src = inv[r * 6 + i]

            @pl.when(src < 0)
            def _(out=out):
                out[i] = jnp.zeros(out.shape[1:], BF16)

            @pl.when(src >= 0)
            def _(out=out, src=src):
                out[i] = de[src]

        return carry

    lax.fori_loop(0, 6, place, 0)


def backward(inv, probs, kb, vb, q, dc, wk, wv):
    width = wk.shape[0]
    return pl.pallas_call(
        backward_kernel,
        in_specs=[SMEM] + [VMEM] * 7,
        out_specs=[VMEM] * 7,
        out_shape=[
            jax.ShapeDtypeStruct(q.shape, BF16),
            jax.ShapeDtypeStruct(kb.shape, BF16),
            jax.ShapeDtypeStruct(kb.shape, BF16),
        ]
        + [jax.ShapeDtypeStruct((6, NLEN, width), BF16)] * 4,
        scratch_shapes=[pltpu.VMEM((2 * KMAX, NLEN, width), BF16)],
        compiler_params=pltpu.CompilerParams(vmem_limit_bytes=48 << 20),
        name="backward",
    )(inv, probs, kb, vb, q, dc, wk, wv)


def unproject_kernel(n_ref, x, w, o):
    for s in range(4):
        block = w[2 * s : 2 * s + 2].reshape(256, 512)
        o[0, :, 256 * s : 256 * s + 256] = dot(x[...], block, NT).astype(BF16)


def unproject(n, x, weights, row):
    tokens = x.shape[0]
    return pl.pallas_call(
        unproject_kernel,
        grid_spec=pltpu.PrefetchScalarGridSpec(
            num_scalar_prefetch=1,
            grid=(4,),
            in_specs=[
                pl.BlockSpec((tokens, 512), lambda r, n: (0, 0)),
                pl.BlockSpec((8, 128, 512), lambda r, n: ((n[0] + r) % 4, row, 0)),
            ],
            out_specs=pl.BlockSpec((1, tokens, 1024), lambda r, n: (r, 0, 0)),
        ),
        out_shape=jax.ShapeDtypeStruct((4, tokens, 1024), BF16),
        compiler_params=pltpu.CompilerParams(vmem_limit_bytes=32 << 20),
        name="unproject",
    )(n, x, weights)


def outer_kernel(n_ref, d, ctx, o):
    for s in range(4):
        o[s] = dot(d[0, :, 256 * s : 256 * s + 256], ctx[...], TN).astype(BF16)


def outer(n, dout, ctx):
    tokens = ctx.shape[0]
    return pl.pallas_call(
        outer_kernel,
        grid_spec=pltpu.PrefetchScalarGridSpec(
            num_scalar_prefetch=1,
            grid=(4,),
            in_specs=[
                pl.BlockSpec((1, tokens, 1024), lambda r, n: (r, 0, 0)),
                pl.BlockSpec((tokens, 512), lambda r, n: (0, 0)),
            ],
            out_specs=pl.BlockSpec((4, 256, 512), lambda r, n: ((n[0] + r) % 4, 0, 0)),
        ),
        out_shape=jax.ShapeDtypeStruct((16, 256, 512), BF16),
        compiler_params=pltpu.CompilerParams(vmem_limit_bytes=32 << 20),
        name="outer",
    )(n, dout, ctx)


def slot_tables(slot_span, n):
    rel = jnp.roll(slot_span.reshape(4, 6), -n, axis=0).reshape(-1)
    slots = rel.shape[0]
    ids = jnp.arange(slots, dtype=jnp.int32)
    before = ids[None, :] < ids[:, None]
    rank = jnp.sum((rel[None, :] == rel[:, None]) & before, axis=1, dtype=jnp.int32)
    where = jnp.where(rel >= 0, rel * KMAX + rank, -1).astype(jnp.int32)
    spot = jnp.arange(2 * KMAX, dtype=jnp.int32)
    hit = where[None, :] == spot[:, None]
    source = jnp.sum(jnp.where(hit, ids[None, :] + 1, 0), axis=1, dtype=jnp.int32) - 1
    counts = jnp.sum(rel[None, :] == jnp.arange(2)[:, None], axis=1, dtype=jnp.int32)
    return jnp.concatenate([source, counts]), where, rel


def body(hidden, d_out, nbr_emb, slot_span, dec_gain, enc_gain, w_cond, w_enc, w_q, w_k, w_v, w_o):
    n = lax.axis_index("nbr")
    b = lax.axis_index("batch")
    n1 = n.astype(jnp.int32).reshape(1)
    tokens, feats = hidden.shape
    spans = tokens // CLEN

    q_half = lax.dynamic_slice_in_dim(w_q, b * 128, 128, axis=0)
    o_half = lax.dynamic_slice_in_dim(w_o, b * 128, 128, axis=1).T
    kv_half = jnp.where(b == 0, w_k, w_v)
    weights = lax.all_gather(
        jnp.concatenate([q_half, o_half, kv_half], axis=0), ("seq", "batch"), axis=0
    )

    pooled = jnp.mean(hidden.astype(F32).reshape(spans, CLEN, feats), axis=1).astype(BF16)
    length = lax.axis_size("seq")
    carried = lax.ppermute(
        pooled[spans - 1 :], "seq", [(i, i + 1) for i in range(length - 1)]
    )
    previous = jnp.concatenate([carried, pooled[: spans - 1]], axis=0)
    condition = sum_small(jnp.dot(previous, w_cond, preferred_element_type=F32))

    e1, e2a, e2b, e3 = ring_gather(nbr_emb)
    gain_rows = jnp.broadcast_to(dec_gain[None], (8, feats))
    half = tokens // 2
    state = jnp.concatenate([hidden[:half], gain_rows, hidden[half:], gain_rows], axis=0)
    state = lax.optimization_barrier((state, e1, e3))[0]
    h1, h2a, h2b, h3 = ring_gather(state)
    d1, d2a, d2b, d3 = ring_gather(lax.optimization_barrier((d_out, e2a, e2b))[0])

    tab, inv, rel_span = slot_tables(slot_span, n)

    def encode(block, first):
        own = lax.slice_in_dim(rel_span, first, first + block.shape[0])
        own = own[:, None, None]
        cond = jnp.where(own == 0, condition[0], jnp.where(own == 1, condition[1], 0.0))
        x = block.astype(F32) + cond
        enc_normed = (x * rms_scale(x) * enc_gain.astype(F32)).astype(BF16)
        width = x.shape[2]
        mixed = jnp.dot(
            enc_normed.reshape(-1, width), w_enc, preferred_element_type=F32
        ).reshape(x.shape)
        return (x + jax.nn.silu(mixed)).astype(BF16)

    encoded = [
        encode(nbr_emb, 0), encode(e1, 6), encode(e2a, 12), encode(e2b, 15), encode(e3, 18)
    ]

    def states(rows):
        return jnp.concatenate([rows[:half], rows[half + 8 : tokens + 8]], axis=0)

    hid_rel = jnp.stack(
        [hidden, states(h1), jnp.concatenate([h2a[:half], h2b[:half]], axis=0), states(h3)]
    )
    gain_rel = jnp.stack([dec_gain, h1[half], h2a[half], h3[half]])
    hf = hid_rel.astype(F32)
    rstd = lax.rsqrt(jnp.mean(hf * hf, axis=(0, 2)) + 1e-06)[:, None]
    normed = (hf * rstd[None] * gain_rel.astype(F32)[:, None, :]).astype(BF16)
    dout_rel = jnp.stack([d_out, d1, jnp.concatenate([d2a, d2b], axis=0), d3])

    pairs = weights.reshape(16, 2, 312, 512)
    wk = pairs[:, 0, 256:].reshape(-1, 512)
    wv = pairs[:, 1, 256:].reshape(-1, 512)

    query = project(n1, normed, weights, 0)
    enc, ctx, probs, keys, values = forward(tab, encoded, wk, wv, query)
    out_sum = ring_scatter_rows(unproject(n1, ctx, weights, 1))

    d_wo_part = outer(n1, dout_rel, ctx)
    d_wo = lax.psum_scatter(d_wo_part, "seq", scatter_dimension=0, tiled=False).astype(F32).T

    d_ctx = project(n1, dout_rel, weights, 1)
    d_query, d_key, d_value, g0, g1, g2, g3 = backward(
        inv, probs, keys, values, query, d_ctx, wk, wv
    )
    d_enc_low, d_enc_high = ring_scatter(g0, g1, g2, g3)
    d_enc = jnp.concatenate([d_enc_low, d_enc_high], axis=0).astype(BF16)
    own_grad = ring_scatter_rows(unproject(n1, d_query, weights, 0))

    rows = enc.reshape(-1, enc.shape[2])
    d_wk_part = dot(rows, d_key, TN).astype(BF16).reshape(16, -1, 512)
    d_wv_part = dot(rows, d_value, TN).astype(BF16).reshape(16, -1, 512)
    shares = lax.all_to_all(
        jnp.concatenate([d_wk_part, d_wv_part], axis=1), "seq", 0, 0, tiled=True
    )
    d_wkv = jnp.sum(shares.astype(F32), axis=0)
    d_wk, d_wv = d_wkv[:56], d_wkv[56:]

    own = hidden.astype(F32)
    out = (own + out_sum).astype(BF16)
    scaled = dec_gain.astype(F32) * own_grad
    stat = sum_small(jnp.sum(own * scaled, axis=-1, keepdims=True) / (4 * feats))
    d_hidden = d_out.astype(F32) + rstd * scaled - own * rstd**3 * stat
    return (out, d_hidden.astype(BF16), d_enc, d_wo, d_wk, d_wv)


def solution(mesh):
    placed = (
        P(("batch", "seq"), "nbr"),
        P(("batch", "seq"), "nbr"),
        P(("batch", "seq", "nbr"), None, None),
        P(("batch", "seq")),
        P("nbr"),
        P(),
        P("nbr", None),
        P(),
        P("seq", "nbr"),
        P("seq", "nbr"),
        P("seq", "nbr"),
        P("nbr", "seq"),
    )
    return jax.shard_map(
        body,
        mesh=mesh,
        in_specs=placed,
        out_specs=(
            P(("batch", "seq"), "nbr"),
            P(("batch", "seq"), "nbr"),
            P(("batch", "seq", "nbr"), None, None),
            P(("batch", "nbr"), "seq"),
            P(("batch", "seq"), "nbr"),
            P(("batch", "seq"), "nbr"),
        ),
        check_vma=False,
    )
```

```python
import jax
import jax.numpy as jnp
from jax import lax
from jax.experimental import pallas as pl
from jax.experimental.pallas import tpu as pltpu
from jax.sharding import PartitionSpec as P

HD = 128
CLEN = 64
NLEN = 128
KMAX = 8
F32 = jnp.float32
BF16 = jnp.bfloat16
VMEM = pl.BlockSpec(memory_space=pltpu.VMEM)
SMEM = pl.BlockSpec(memory_space=pltpu.SMEM)


def dot(a, b, dims=((1,), (0,))):
    return lax.dot_general(a, b, (dims, ((), ())), preferred_element_type=F32)


NT = ((1,), (1,))
TN = ((0,), (0,))


def shift(x, by):
    n = lax.axis_size("nbr")
    return lax.ppermute(x, "nbr", [(i, (i + by) % n) for i in range(n)])


def ring_gather(x):
    half = x.shape[0] // 2
    right = shift(x, -1)
    left = shift(x, 1)
    far_a = shift(right[:half], -1)
    far_b = shift(left[half:], 1)
    return right, far_a, far_b, left


def scattered(parts):
    return [parts[0]] + [shift(parts[r], r) for r in (2, 1, 3)]


def total(shares):
    return sum(x.astype(F32) for x in shares)


def sum_small(x):
    return x + shift(x, 1) + shift(x, 2) + shift(x, 3)


def exchange(parts):
    return lax.all_to_all(parts, "seq", split_axis=0, concat_axis=0, tiled=True)


def rms_scale(values):
    return lax.rsqrt(jnp.mean(values * values, axis=-1, keepdims=True) + 1e-06)


def cost(products, moved):
    return pl.CostEstimate(flops=2 * products, transcendentals=0, bytes_accessed=moved)


def project_kernel(n_ref, x_ref, w, o_ref, acc):
    step = pl.program_id(0)
    x = x_ref[0]
    part = jnp.zeros(acc.shape, F32)
    for s in range(4):
        block = w[2 * s : 2 * s + 2].reshape(256, 512)
        part += dot(x[:, 256 * s : 256 * s + 256], block)

    @pl.when(step == 0)
    def _():
        acc[...] = part

    @pl.when((step > 0) & (step < 3))
    def _():
        acc[...] += part

    @pl.when(step == 3)
    def _():
        o_ref[...] = (acc[...] + part).astype(BF16)


def project(n, x, weights, row):
    tokens = x.shape[1]
    return pl.pallas_call(
        project_kernel,
        grid_spec=pltpu.PrefetchScalarGridSpec(
            num_scalar_prefetch=1,
            grid=(4,),
            in_specs=[
                pl.BlockSpec((1, tokens, 1024), lambda r, n: (r, 0, 0)),
                pl.BlockSpec((8, 128, 512), lambda r, n: ((n[0] + r) % 4, row, 0)),
            ],
            out_specs=pl.BlockSpec((tokens, 512), lambda r, n: (0, 0)),
            scratch_shapes=[pltpu.VMEM((tokens, 512), F32)],
        ),
        out_shape=jax.ShapeDtypeStruct((tokens, 512), BF16),
        cost_estimate=cost(tokens * 4096 * 512, 6 << 20),
        compiler_params=pltpu.CompilerParams(vmem_limit_bytes=24 << 20),
        name="project",
    )(n, x, weights)


def forward_kernel(tab, e0, e1, e2a, e2b, e3, wk, wv, q, enc, ctx, probs, kb, vb):
    half = e2a.shape[0]
    tables = ((e0, 0), (e1, 6), (e2a, 12), (e2b, 12 + half), (e3, 18))

    def pick(j, carry):
        src = tab[j]

        @pl.when(src < 0)
        def _():
            enc[j] = jnp.zeros(enc.shape[1:], BF16)

        for ref, first in tables:

            @pl.when((src >= first) & (src < first + ref.shape[0]))
            def _(ref=ref, first=first):
                enc[j] = ref[src - first]

        return carry

    lax.fori_loop(0, 2 * KMAX, pick, 0)

    def kv(c, carry):
        x = enc[pl.ds(4 * c, 4)].reshape(4 * NLEN, enc.shape[2])
        rows = pl.ds(pl.multiple_of(c * 512, 512), 512)
        kb[rows, :] = dot(x, wk[...]).astype(BF16)
        vb[rows, :] = dot(x, wv[...]).astype(BF16)
        return carry

    lax.fori_loop(0, 4, kv, 0)
    factor = HD ** (-0.5)
    heads = q.shape[1] // HD
    keys = KMAX * NLEN
    for c in range(2):
        limit = tab[2 * KMAX + c] * NLEN
        allowed = lax.broadcasted_iota(jnp.int32, (CLEN, keys), 1) < limit
        toks = slice(c * CLEN, (c + 1) * CLEN)
        rows = slice(c * keys, (c + 1) * keys)
        for h in range(heads):
            cols = slice(h * HD, (h + 1) * HD)
            s = jnp.where(allowed, dot(q[toks, cols], kb[rows, cols], NT) * factor, -1e30)
            w = jnp.exp(s - jnp.max(s, axis=-1, keepdims=True))
            p = w / jnp.sum(w, axis=-1, keepdims=True)
            probs[c * heads + h] = p
            ctx[toks, cols] = dot(p.astype(BF16), vb[rows, cols]).astype(BF16)


def forward(tab, blocks, wk, wv, q):
    rows = 2 * KMAX * NLEN
    flat = jax.ShapeDtypeStruct((rows, q.shape[1]), BF16)
    probs = jax.ShapeDtypeStruct((2 * q.shape[1] // HD, CLEN, KMAX * NLEN), F32)
    return pl.pallas_call(
        forward_kernel,
        in_specs=[SMEM] + [VMEM] * 8,
        out_specs=[VMEM] * 5,
        out_shape=[
            jax.ShapeDtypeStruct((2 * KMAX, NLEN, wk.shape[0]), BF16),
            jax.ShapeDtypeStruct(q.shape, BF16),
            probs,
            flat,
            flat,
        ],
        cost_estimate=cost(2048 * 896 * 1024, 36 << 20),
        compiler_params=pltpu.CompilerParams(vmem_limit_bytes=32 << 20),
        name="forward",
    )(tab, *blocks, wk, wv, q)


def backward_kernel(inv, probs, kb, vb, q, dc, wk, wv, dq, dk, dv, out, de):
    factor = HD ** (-0.5)
    heads = q.shape[1] // HD
    keys = KMAX * NLEN
    for c in range(2):
        toks = slice(c * CLEN, (c + 1) * CLEN)
        rows = slice(c * keys, (c + 1) * keys)
        for h in range(heads):
            cols = slice(h * HD, (h + 1) * HD)
            dh = dc[toks, cols]
            p = probs[c * heads + h]
            dp = dot(dh, vb[rows, cols], NT)
            rd = jnp.sum(p * dp, axis=-1, keepdims=True)
            ds = (p * (dp - rd) * factor).astype(BF16)
            dq[toks, cols] = dot(ds, kb[rows, cols]).astype(BF16)
            dk[rows, cols] = dot(ds, q[toks, cols], TN).astype(BF16)
            dv[rows, cols] = dot(p.astype(BF16), dh, TN).astype(BF16)

    def grad(c, carry):
        rows = pl.ds(pl.multiple_of(c * 512, 512), 512)
        part = dot(dk[rows, :], wk[...], NT) + dot(dv[rows, :], wv[...], NT)
        de[pl.ds(4 * c, 4)] = part.astype(BF16).reshape(4, NLEN, wk.shape[0])
        return carry

    lax.fori_loop(0, 4, grad, 0)

    def place(i, carry):
        src = inv[i]

        @pl.when(src < 0)
        def _():
            out[i] = jnp.zeros(out.shape[1:], BF16)

        @pl.when(src >= 0)
        def _():
            out[i] = de[src]

        return carry

    lax.fori_loop(0, out.shape[0], place, 0)


def backward(inv, probs, kb, vb, q, dc, wk, wv):
    width = wk.shape[0]
    return pl.pallas_call(
        backward_kernel,
        in_specs=[SMEM] + [VMEM] * 7,
        out_specs=[VMEM] * 4,
        out_shape=[
            jax.ShapeDtypeStruct(q.shape, BF16),
            jax.ShapeDtypeStruct(kb.shape, BF16),
            jax.ShapeDtypeStruct(kb.shape, BF16),
        ]
        + [jax.ShapeDtypeStruct((inv.shape[0], NLEN, width), BF16)],
        scratch_shapes=[pltpu.VMEM((2 * KMAX, NLEN, width), BF16)],
        cost_estimate=cost(2048 * 896 * 1024, 40 << 20),
        compiler_params=pltpu.CompilerParams(vmem_limit_bytes=34 << 20),
        name="backward",
    )(inv, probs, kb, vb, q, dc, wk, wv)


def unproject_kernel(n_ref, x, more, w, o):
    tokens = x.shape[0]
    for s in range(4):
        block = w[2 * s : 2 * s + 2].reshape(256, 512)
        o[0, :tokens, 256 * s : 256 * s + 256] = dot(x[...], block, NT).astype(BF16)
    if o.shape[1] > tokens:
        o[0, tokens:, :] = more[...]


def unproject(n, x, weights, row, more=None):
    tokens = x.shape[0]
    rows = tokens
    if more is None:
        more = jnp.zeros((16, 1024), BF16)
    else:
        rows += more.shape[0]
    return pl.pallas_call(
        unproject_kernel,
        grid_spec=pltpu.PrefetchScalarGridSpec(
            num_scalar_prefetch=1,
            grid=(4,),
            in_specs=[
                pl.BlockSpec((tokens, 512), lambda r, n: (0, 0)),
                pl.BlockSpec((16, 1024), lambda r, n: (0, 0)),
                pl.BlockSpec((8, 128, 512), lambda r, n: ((n[0] + r) % 4, row, 0)),
            ],
            out_specs=pl.BlockSpec((1, rows, 1024), lambda r, n: (r, 0, 0)),
        ),
        out_shape=jax.ShapeDtypeStruct((4, rows, 1024), BF16),
        cost_estimate=cost(tokens * 4096 * 512, 6 << 20),
        compiler_params=pltpu.CompilerParams(vmem_limit_bytes=24 << 20),
        name="unproject",
    )(n, x, more, weights)


def outer_kernel(at, d, ctx, a0, a1, a2, a3, b0, b1, b2, b3):
    n, x, z = at[0], at[1], at[2]
    upper, lower = (a0, a1, a2, a3), (b0, b1, b2, b3)
    half = a0.shape[1]
    for i in range(4):
        block = lax.rem(x + i + 4 - n, 4)
        for j in range(4):
            first = pl.multiple_of(lax.rem(z + j, 4) * 2 * half, 2 * half)
            part = dot(d[block, :, pl.ds(first, 2 * half)], ctx[...], TN).astype(BF16)
            upper[i][j] = part[:half]
            lower[j][i] = part[half:]


def outer(at, dout, ctx):
    share = jax.ShapeDtypeStruct((4, 128, ctx.shape[1]), BF16)
    return pl.pallas_call(
        outer_kernel,
        in_specs=[SMEM, VMEM, VMEM],
        out_specs=[VMEM] * 8,
        out_shape=[share] * 8,
        cost_estimate=cost(ctx.shape[0] * 4096 * 512, 6 << 20),
        compiler_params=pltpu.CompilerParams(vmem_limit_bytes=24 << 20),
        name="outer",
    )(at, dout, ctx)


def along_x(share, by):
    return lax.ppermute(share, "seq", [(i, (i // 4 + by) % 4 * 4 + i % 4) for i in range(16)])


def along_z(share, by):
    return lax.ppermute(share, "seq", [(i, i // 4 * 4 + (i + by) % 4) for i in range(16)])


def slot_tables(slot_span, n):
    slots = slot_span.shape[0]
    ids = jnp.arange(slots, dtype=jnp.int32)
    before = ids[None, :] < ids[:, None]
    same = slot_span[None, :] == slot_span[:, None]
    rank = jnp.sum(same & before, axis=1, dtype=jnp.int32)
    where = jnp.where(slot_span >= 0, slot_span * KMAX + rank, -1).astype(jnp.int32)
    spot = jnp.arange(2 * KMAX, dtype=jnp.int32)
    hit = where[None, :] == spot[:, None]
    relative = (ids + slots - 6 * n) % slots
    source = jnp.sum(jnp.where(hit, relative[None, :] + 1, 0), axis=1, dtype=jnp.int32) - 1
    counts = jnp.sum(slot_span[None, :] == jnp.arange(2)[:, None], axis=1, dtype=jnp.int32)
    return jnp.concatenate([source, counts]), where


def body(hidden, d_out, nbr_emb, slot_span, dec_gain, enc_gain, w_cond, w_enc, w_q, w_k, w_v, w_o):
    n = lax.axis_index("nbr")
    b = lax.axis_index("batch")
    n1 = n.astype(jnp.int32).reshape(1)
    tokens, feats = hidden.shape
    spans = tokens // CLEN

    q_half = lax.dynamic_slice_in_dim(w_q, b * 128, 128, axis=0)
    o_half = lax.dynamic_slice_in_dim(w_o, b * 128, 128, axis=1).T
    kv_half = jnp.where(b == 0, w_k, w_v)
    weights = lax.all_gather(
        jnp.concatenate([q_half, o_half, kv_half], axis=0), ("seq", "batch"), axis=0
    )

    gain_rows = jnp.broadcast_to(dec_gain[None], (8, feats))
    half = tokens // 2
    state = jnp.concatenate([hidden[:half], gain_rows, hidden[half:], gain_rows], axis=0)
    h1, h2a, h2b, h3 = ring_gather(state)

    pooled = jnp.mean(hidden.astype(F32).reshape(spans, CLEN, feats), axis=1).astype(BF16)
    length = lax.axis_size("seq")
    carried = lax.ppermute(
        pooled[spans - 1 :], "seq", [(i, i + 1) for i in range(length - 1)]
    )
    previous = jnp.concatenate([carried, pooled[: spans - 1]], axis=0)
    condition = sum_small(jnp.dot(previous, w_cond, preferred_element_type=F32))

    nbr_emb = lax.optimization_barrier((nbr_emb, condition))[0]
    e1, e2a, e2b, e3 = ring_gather(nbr_emb)
    later = lax.optimization_barrier((d_out, e2a, e2b, weights))
    weights = later[3]
    d2, d1, d3 = (shift(later[0], r) for r in (2, -1, 1))

    tab, inv = slot_tables(slot_span, n)
    rel_span = jnp.roll(slot_span.reshape(4, 6), -n, axis=0).reshape(-1)

    def encode(block, first):
        own = lax.slice_in_dim(rel_span, first, first + block.shape[0])
        own = own[:, None, None]
        cond = jnp.where(own == 0, condition[0], jnp.where(own == 1, condition[1], 0.0))
        x = block.astype(F32) + cond
        enc_normed = (x * rms_scale(x) * enc_gain.astype(F32)).astype(BF16)
        width = x.shape[2]
        mixed = jnp.dot(
            enc_normed.reshape(-1, width), w_enc, preferred_element_type=F32
        ).reshape(x.shape)
        return (x + jax.nn.silu(mixed)).astype(BF16)

    encoded = [
        encode(nbr_emb, 0), encode(e1, 6), encode(e2a, 12), encode(e2b, 15), encode(e3, 18)
    ]

    def states(rows):
        return jnp.concatenate([rows[:half], rows[half + 8 : tokens + 8]], axis=0)

    hid_rel = jnp.stack(
        [hidden, states(h1), jnp.concatenate([h2a[:half], h2b[:half]], axis=0), states(h3)]
    )
    gain_rel = jnp.stack([dec_gain, h1[half], h2a[half], h3[half]])
    hf = hid_rel.astype(F32)
    rstd = lax.rsqrt(jnp.mean(hf * hf, axis=(0, 2)) + 1e-06)[:, None]
    normed = (hf * rstd[None] * gain_rel.astype(F32)[:, None, :]).astype(BF16)
    dout_rel = jnp.stack([d_out, d1, d2, d3])

    pairs = weights.reshape(16, 2, 312, 512)
    weights = pltpu.with_memory_space_constraint(weights, pltpu.HBM)
    wk = pairs[:, 0, 256:].reshape(-1, 512)
    wv = pairs[:, 1, 256:].reshape(-1, 512)

    query = project(n1, normed, weights, 0)
    enc, ctx, probs, keys, values = forward(tab, encoded, wk, wv, query)
    out_parts = unproject(n1, ctx, weights, 1)
    out_shares = scattered(out_parts)

    place = lax.axis_index("seq").astype(jnp.int32)
    at = jnp.stack([n.astype(jnp.int32), place // 4, place % 4])
    d_wo_parts = outer(at, dout_rel, ctx)
    upper = [along_x(d_wo_parts[i], i) for i in (2, 1, 3)]
    lower = [along_z(d_wo_parts[4 + i], i) for i in (2, 1, 3)]

    d_ctx = project(n1, dout_rel, weights, 1)
    d_ctx = lax.optimization_barrier((d_ctx, out_parts, d_wo_parts))[0]
    d_query, d_key, d_value, parts = backward(
        inv, probs, keys, values, query, d_ctx, wk, wv
    )
    parts, out_shares, upper, lower = lax.optimization_barrier(
        (parts, out_shares, upper, lower)
    )
    upper = total([d_wo_parts[0]] + upper).astype(BF16)
    lower = total([d_wo_parts[4]] + lower).astype(BF16)
    upper = total([upper[0]] + [along_z(upper[i], i) for i in (2, 1, 3)])
    lower = total([lower[0]] + [along_x(lower[i], i) for i in (2, 1, 3)])
    d_wo = jnp.concatenate([upper, lower], axis=0).T
    d_enc = lax.psum_scatter(parts, "nbr", scatter_dimension=0, tiled=True)

    inner = jnp.sum(d_query.astype(F32) * query.astype(F32), axis=-1).astype(BF16)
    more = jnp.broadcast_to(jnp.pad(inner, (0, feats - tokens))[None], (16, feats))
    own_grad = total(scattered(unproject(n1, d_query, weights, 0, more)))
    stat = own_grad[tokens, :tokens][:, None] / (rstd * (4 * feats))
    own_grad = own_grad[:tokens]

    rows = enc.reshape(-1, enc.shape[2])
    d_wk_part = dot(rows, d_key, TN).astype(BF16).reshape(16, -1, 512)
    d_wv_part = dot(rows, d_value, TN).astype(BF16).reshape(16, -1, 512)
    d_wkv_parts = jnp.concatenate([d_wk_part, d_wv_part], axis=1)
    d_wkv = jnp.sum(exchange(d_wkv_parts).astype(F32), axis=0)
    d_wk, d_wv = d_wkv[:56], d_wkv[56:]

    own = hidden.astype(F32)
    out = (own + total(out_shares)).astype(BF16)
    scaled = dec_gain.astype(F32) * own_grad
    d_hidden = d_out.astype(F32) + rstd * scaled - own * rstd**3 * stat
    return (out, d_hidden.astype(BF16), d_enc, d_wo, d_wk, d_wv)


def solution(mesh):
    placed = (
        P(("batch", "seq"), "nbr"),
        P(("batch", "seq"), "nbr"),
        P(("batch", "seq", "nbr"), None, None),
        P(("batch", "seq")),
        P("nbr"),
        P(),
        P("nbr", None),
        P(),
        P("seq", "nbr"),
        P("seq", "nbr"),
        P("seq", "nbr"),
        P("nbr", "seq"),
    )
    return jax.shard_map(
        body,
        mesh=mesh,
        in_specs=placed,
        out_specs=(
            P(("batch", "seq"), "nbr"),
            P(("batch", "seq"), "nbr"),
            P(("batch", "seq", "nbr"), None, None),
            P(("batch", "nbr"), "seq"),
            P(("batch", "seq"), "nbr"),
            P(("batch", "seq"), "nbr"),
        ),
        check_vma=False,
    )
```

```python
import jax
import jax.numpy as jnp
from jax import lax
from jax.experimental import pallas as pl
from jax.experimental.pallas import tpu as pltpu
from jax.sharding import PartitionSpec as P

HD = 128
CLEN = 64
NLEN = 128
KMAX = 8
F32 = jnp.float32
BF16 = jnp.bfloat16
VMEM = pl.BlockSpec(memory_space=pltpu.VMEM)
SMEM = pl.BlockSpec(memory_space=pltpu.SMEM)


def dot(a, b, dims=((1,), (0,))):
    return lax.dot_general(a, b, (dims, ((), ())), preferred_element_type=F32)


NT = ((1,), (1,))
TN = ((0,), (0,))


def shift(x, by):
    n = lax.axis_size("nbr")
    return lax.ppermute(x, "nbr", [(i, (i + by) % n) for i in range(n)])


def ring_gather(x):
    half = x.shape[0] // 2
    right = shift(x, -1)
    left = shift(x, 1)
    far_a = shift(right[:half], -1)
    far_b = shift(left[half:], 1)
    return right, far_a, far_b, left


def scattered(parts):
    return [parts[0]] + [shift(parts[r], r) for r in (2, 1, 3)]


def total(shares):
    return sum(x.astype(F32) for x in shares)


def sum_small(x):
    return x + shift(x, 1) + shift(x, 2) + shift(x, 3)


def exchange(parts):
    return lax.all_to_all(parts, "seq", split_axis=0, concat_axis=0, tiled=True)


def rms_scale(values):
    return lax.rsqrt(jnp.mean(values * values, axis=-1, keepdims=True) + 1e-06)


def cost(products, moved):
    return pl.CostEstimate(flops=2 * products, transcendentals=0, bytes_accessed=moved)


def project_kernel(n_ref, x_ref, w, o_ref, acc):
    step = pl.program_id(0)
    x = x_ref[0]
    part = jnp.zeros(acc.shape, F32)
    for s in range(4):
        block = w[2 * s : 2 * s + 2].reshape(256, 512)
        part += dot(x[:, 256 * s : 256 * s + 256], block)

    @pl.when(step == 0)
    def _():
        acc[...] = part

    @pl.when((step > 0) & (step < 3))
    def _():
        acc[...] += part

    @pl.when(step == 3)
    def _():
        o_ref[...] = (acc[...] + part).astype(BF16)


def project(n, x, weights, row):
    tokens = x.shape[1]
    return pl.pallas_call(
        project_kernel,
        grid_spec=pltpu.PrefetchScalarGridSpec(
            num_scalar_prefetch=1,
            grid=(4,),
            in_specs=[
                pl.BlockSpec((1, tokens, 1024), lambda r, n: (r, 0, 0)),
                pl.BlockSpec((8, 128, 512), lambda r, n: ((n[0] + r) % 4, row, 0)),
            ],
            out_specs=pl.BlockSpec((tokens, 512), lambda r, n: (0, 0)),
            scratch_shapes=[pltpu.VMEM((tokens, 512), F32)],
        ),
        out_shape=jax.ShapeDtypeStruct((tokens, 512), BF16),
        cost_estimate=cost(tokens * 4096 * 512, 6 << 20),
        compiler_params=pltpu.CompilerParams(vmem_limit_bytes=24 << 20),
        name="project",
    )(n, x, weights)


def forward_kernel(tab, e0, e1, e2, e3, wk, wv, q, enc, ctx, probs, kb, vb):
    tables = ((e0, 0), (e1, 6), (e2, 12), (e3, 18))

    def pick(j, carry):
        src = tab[j]

        @pl.when(src < 0)
        def _():
            enc[j] = jnp.zeros(enc.shape[1:], BF16)

        for ref, first in tables:

            @pl.when((src >= first) & (src < first + ref.shape[0]))
            def _(ref=ref, first=first):
                enc[j] = ref[src - first]

        return carry

    lax.fori_loop(0, 2 * KMAX, pick, 0)

    def kv(c, carry):
        x = enc[pl.ds(4 * c, 4)].reshape(4 * NLEN, enc.shape[2])
        rows = pl.ds(pl.multiple_of(c * 512, 512), 512)
        kb[rows, :] = dot(x, wk[...]).astype(BF16)
        vb[rows, :] = dot(x, wv[...]).astype(BF16)
        return carry

    lax.fori_loop(0, 4, kv, 0)
    factor = HD ** (-0.5)
    heads = q.shape[1] // HD
    keys = KMAX * NLEN
    for c in range(2):
        limit = tab[2 * KMAX + c] * NLEN
        allowed = lax.broadcasted_iota(jnp.int32, (CLEN, keys), 1) < limit
        toks = slice(c * CLEN, (c + 1) * CLEN)
        rows = slice(c * keys, (c + 1) * keys)
        for h in range(heads):
            cols = slice(h * HD, (h + 1) * HD)
            s = jnp.where(allowed, dot(q[toks, cols], kb[rows, cols], NT) * factor, -1e30)
            w = jnp.exp(s - jnp.max(s, axis=-1, keepdims=True))
            p = w / jnp.sum(w, axis=-1, keepdims=True)
            probs[c * heads + h] = p
            ctx[toks, cols] = dot(p.astype(BF16), vb[rows, cols]).astype(BF16)


def forward(tab, blocks, wk, wv, q):
    rows = 2 * KMAX * NLEN
    flat = jax.ShapeDtypeStruct((rows, q.shape[1]), BF16)
    probs = jax.ShapeDtypeStruct((2 * q.shape[1] // HD, CLEN, KMAX * NLEN), F32)
    return pl.pallas_call(
        forward_kernel,
        in_specs=[SMEM] + [VMEM] * 7,
        out_specs=[VMEM] * 5,
        out_shape=[
            pltpu.HBM((2 * KMAX, NLEN, wk.shape[0]), BF16),
            jax.ShapeDtypeStruct(q.shape, BF16),
            probs,
            flat,
            flat,
        ],
        cost_estimate=cost(2048 * 896 * 1024, 36 << 20),
        compiler_params=pltpu.CompilerParams(vmem_limit_bytes=32 << 20),
        name="forward",
    )(tab, *blocks, wk, wv, q)


def backward_kernel(inv, probs, kb, vb, q, dc, wk, wv, dq, dk, dv, out, de):
    factor = HD ** (-0.5)
    heads = q.shape[1] // HD
    keys = KMAX * NLEN
    for c in range(2):
        toks = slice(c * CLEN, (c + 1) * CLEN)
        rows = slice(c * keys, (c + 1) * keys)
        for h in range(heads):
            cols = slice(h * HD, (h + 1) * HD)
            dh = dc[toks, cols]
            p = probs[c * heads + h]
            dp = dot(dh, vb[rows, cols], NT)
            rd = jnp.sum(p * dp, axis=-1, keepdims=True)
            ds = (p * (dp - rd) * factor).astype(BF16)
            dq[toks, cols] = dot(ds, kb[rows, cols]).astype(BF16)
            dk[rows, cols] = dot(ds, q[toks, cols], TN).astype(BF16)
            dv[rows, cols] = dot(p.astype(BF16), dh, TN).astype(BF16)

    def grad(c, carry):
        rows = pl.ds(pl.multiple_of(c * 512, 512), 512)
        part = dot(dk[rows, :], wk[...], NT) + dot(dv[rows, :], wv[...], NT)
        de[pl.ds(4 * c, 4)] = part.astype(BF16).reshape(4, NLEN, wk.shape[0])
        return carry

    lax.fori_loop(0, 4, grad, 0)

    def place(i, carry):
        src = inv[i]

        @pl.when(src < 0)
        def _():
            out[i] = jnp.zeros(out.shape[1:], BF16)

        @pl.when(src >= 0)
        def _():
            out[i] = de[src]

        return carry

    lax.fori_loop(0, out.shape[0], place, 0)


def backward(inv, probs, kb, vb, q, dc, wk, wv):
    width = wk.shape[0]
    return pl.pallas_call(
        backward_kernel,
        in_specs=[SMEM] + [VMEM] * 7,
        out_specs=[VMEM] * 4,
        out_shape=[
            jax.ShapeDtypeStruct(q.shape, BF16),
            pltpu.HBM(kb.shape, BF16),
            pltpu.HBM(kb.shape, BF16),
            pltpu.HBM((inv.shape[0], NLEN, width), BF16),
        ],
        scratch_shapes=[pltpu.VMEM((2 * KMAX, NLEN, width), BF16)],
        cost_estimate=cost(2048 * 896 * 1024, 40 << 20),
        compiler_params=pltpu.CompilerParams(vmem_limit_bytes=34 << 20),
        name="backward",
    )(inv, probs, kb, vb, q, dc, wk, wv)


def unproject_kernel(n_ref, ctx, dq, more, w, o):
    tokens = ctx.shape[0]
    for s in range(4):
        cols = slice(256 * s, 256 * s + 256)
        wq = w[2 * s : 2 * s + 2, :128].reshape(256, 512)
        wo = w[2 * s : 2 * s + 2, 128:].reshape(256, 512)
        o[0, :tokens, cols] = dot(ctx[...], wo, NT).astype(BF16)
        o[0, tokens : 2 * tokens, cols] = dot(dq[...], wq, NT).astype(BF16)
    o[0, 2 * tokens :, :] = more[...]


def unproject(n, ctx, dq, more, weights):
    tokens = ctx.shape[0]
    rows = 2 * tokens + more.shape[0]
    return pl.pallas_call(
        unproject_kernel,
        grid_spec=pltpu.PrefetchScalarGridSpec(
            num_scalar_prefetch=1,
            grid=(4,),
            in_specs=[
                pl.BlockSpec((tokens, 512), lambda r, n: (0, 0)),
                pl.BlockSpec((tokens, 512), lambda r, n: (0, 0)),
                pl.BlockSpec(more.shape, lambda r, n: (0, 0)),
                pl.BlockSpec((8, 256, 512), lambda r, n: ((n[0] + r) % 4, 0, 0)),
            ],
            out_specs=pl.BlockSpec((1, rows, 1024), lambda r, n: (r, 0, 0)),
        ),
        out_shape=jax.ShapeDtypeStruct((4, rows, 1024), BF16),
        cost_estimate=cost(2 * tokens * 4096 * 512, 12 << 20),
        compiler_params=pltpu.CompilerParams(vmem_limit_bytes=24 << 20),
        name="unproject",
    )(n, ctx, dq, more, weights)


def outer_kernel(at, d, ctx, a0, a1, a2, a3, b0, b1, b2, b3):
    n, x, z = at[0], at[1], at[2]
    upper, lower = (a0, a1, a2, a3), (b0, b1, b2, b3)
    half = a0.shape[1]
    for i in range(4):
        block = lax.rem(x + i + 4 - n, 4)
        for j in range(4):
            first = pl.multiple_of(lax.rem(z + j, 4) * 2 * half, 2 * half)
            part = dot(d[block, :, pl.ds(first, 2 * half)], ctx[...], TN).astype(BF16)
            upper[i][j] = part[:half]
            lower[j][i] = part[half:]


def outer(at, dout, ctx):
    share = jax.ShapeDtypeStruct((4, 128, ctx.shape[1]), BF16)
    return pl.pallas_call(
        outer_kernel,
        in_specs=[SMEM, VMEM, VMEM],
        out_specs=[VMEM] * 8,
        out_shape=[share] * 8,
        cost_estimate=cost(ctx.shape[0] * 4096 * 512, 6 << 20),
        compiler_params=pltpu.CompilerParams(vmem_limit_bytes=24 << 20),
        name="outer",
    )(at, dout, ctx)


def along_x(share, by):
    return lax.ppermute(share, "seq", [(i, (i // 4 + by) % 4 * 4 + i % 4) for i in range(16)])


def along_z(share, by):
    return lax.ppermute(share, "seq", [(i, i // 4 * 4 + (i + by) % 4) for i in range(16)])


def slot_tables(slot_span, n):
    slots = slot_span.shape[0]
    ids = jnp.arange(slots, dtype=jnp.int32)
    before = ids[None, :] < ids[:, None]
    same = slot_span[None, :] == slot_span[:, None]
    rank = jnp.sum(same & before, axis=1, dtype=jnp.int32)
    where = jnp.where(slot_span >= 0, slot_span * KMAX + rank, -1).astype(jnp.int32)
    spot = jnp.arange(2 * KMAX, dtype=jnp.int32)
    hit = where[None, :] == spot[:, None]
    relative = (ids + slots - 6 * n) % slots
    source = jnp.sum(jnp.where(hit, relative[None, :] + 1, 0), axis=1, dtype=jnp.int32) - 1
    counts = jnp.sum(slot_span[None, :] == jnp.arange(2)[:, None], axis=1, dtype=jnp.int32)
    return jnp.concatenate([source, counts]), where


def body(hidden, d_out, nbr_emb, slot_span, dec_gain, enc_gain, w_cond, w_enc, w_q, w_k, w_v, w_o):
    n = lax.axis_index("nbr")
    b = lax.axis_index("batch")
    n1 = n.astype(jnp.int32).reshape(1)
    tokens, feats = hidden.shape
    spans = tokens // CLEN

    q_half = lax.dynamic_slice_in_dim(w_q, b * 128, 128, axis=0)
    o_half = lax.dynamic_slice_in_dim(w_o, b * 128, 128, axis=1).T
    kv_half = jnp.where(b == 0, w_k, w_v)
    weights = lax.all_gather(
        jnp.concatenate([q_half, o_half, kv_half], axis=0), ("seq", "batch"), axis=0
    )

    gain_rows = jnp.broadcast_to(dec_gain[None], (8, feats))
    half = tokens // 2
    state = jnp.concatenate([hidden[:half], gain_rows, hidden[half:], gain_rows], axis=0)
    h1, h2a, h2b, h3 = ring_gather(state)

    pooled = jnp.mean(hidden.astype(F32).reshape(spans, CLEN, feats), axis=1).astype(BF16)
    length = lax.axis_size("seq")
    carried = lax.ppermute(
        pooled[spans - 1 :], "seq", [(i, i + 1) for i in range(length - 1)]
    )
    previous = jnp.concatenate([carried, pooled[: spans - 1]], axis=0)
    condition = sum_small(jnp.dot(previous, w_cond, preferred_element_type=F32))

    nbr_emb = lax.optimization_barrier((nbr_emb, condition))[0]
    e1, e2a, e2b, e3 = ring_gather(nbr_emb)
    later = lax.optimization_barrier((d_out, e2a, e2b, weights))
    weights = later[3]
    d2, d1, d3 = (shift(later[0], r) for r in (2, -1, 1))

    tab, inv = slot_tables(slot_span, n)
    rel_span = jnp.roll(slot_span.reshape(4, 6), -n, axis=0).reshape(-1)

    def encode(block, first):
        own = lax.slice_in_dim(rel_span, first, first + block.shape[0])
        own = own[:, None, None]
        cond = jnp.where(own == 0, condition[0], jnp.where(own == 1, condition[1], 0.0))
        x = block.astype(F32) + cond
        enc_normed = (x * rms_scale(x) * enc_gain.astype(F32)).astype(BF16)
        width = x.shape[2]
        mixed = jnp.dot(
            enc_normed.reshape(-1, width), w_enc, preferred_element_type=F32
        ).reshape(x.shape)
        return (x + jax.nn.silu(mixed)).astype(BF16)


    def states(rows):
        return jnp.concatenate([rows[:half], rows[half + 8 : tokens + 8]], axis=0)

    hid_rel = jnp.stack(
        [hidden, states(h1), jnp.concatenate([h2a[:half], h2b[:half]], axis=0), states(h3)]
    )
    gain_rel = jnp.stack([dec_gain, h1[half], h2a[half], h3[half]])
    hf = hid_rel.astype(F32)
    rstd = lax.rsqrt(jnp.mean(hf * hf, axis=(0, 2)) + 1e-06)[:, None]
    normed = (hf * rstd[None] * gain_rel.astype(F32)[:, None, :]).astype(BF16)
    dout_rel = jnp.stack([d_out, d1, d2, d3])

    pairs = weights.reshape(16, 2, 312, 512)
    weights = pltpu.with_memory_space_constraint(weights, pltpu.HBM)
    wk = pairs[:, 0, 256:].reshape(-1, 512)
    wv = pairs[:, 1, 256:].reshape(-1, 512)

    query = project(n1, normed, weights, 0)
    e2, query, wk, wv = lax.optimization_barrier(
        (jnp.concatenate([e2a, e2b], axis=0), query, wk, wv)
    )
    encoded = [encode(nbr_emb, 0), encode(e1, 6), encode(e2, 12), encode(e3, 18)]
    enc, ctx, probs, keys, values = forward(tab, encoded, wk, wv, query)
    d_ctx = project(n1, dout_rel, weights, 1)
    d_query, d_key, d_value, parts = backward(
        inv, probs, keys, values, query, d_ctx, wk, wv
    )
    d_enc = lax.psum_scatter(parts, "nbr", scatter_dimension=0, tiled=True)
    ctx = lax.optimization_barrier((ctx, d_query))[0]

    place = lax.axis_index("seq").astype(jnp.int32)
    at = jnp.stack([n.astype(jnp.int32), place // 4, place % 4])
    d_wo_parts = outer(at, dout_rel, ctx)
    upper = [along_x(d_wo_parts[i], i) for i in (2, 1, 3)]
    lower = [along_z(d_wo_parts[4 + i], i) for i in (2, 1, 3)]
    upper = total([d_wo_parts[0]] + upper).astype(BF16)
    lower = total([d_wo_parts[4]] + lower).astype(BF16)
    upper = total([upper[0]] + [along_z(upper[i], i) for i in (2, 1, 3)])
    lower = total([lower[0]] + [along_x(lower[i], i) for i in (2, 1, 3)])
    d_wo = jnp.concatenate([upper, lower], axis=0).T

    inner = jnp.sum(d_query.astype(F32) * query.astype(F32), axis=-1).astype(BF16)
    more = jnp.broadcast_to(jnp.pad(inner, (0, feats - tokens))[None], (16, feats))
    sums = total(scattered(unproject(n1, ctx, d_query, more, weights)))
    out_sum, own_grad = sums[:tokens], sums[tokens : 2 * tokens]
    stat = sums[2 * tokens, :tokens][:, None] / (rstd * (4 * feats))

    rows = enc.reshape(-1, enc.shape[2])
    d_wk_part = dot(rows, d_key, TN).astype(BF16).reshape(16, -1, 512)
    d_wv_part = dot(rows, d_value, TN).astype(BF16).reshape(16, -1, 512)
    d_wkv_parts = jnp.concatenate([d_wk_part, d_wv_part], axis=1)
    d_wkv = jnp.sum(exchange(d_wkv_parts).astype(F32), axis=0)
    d_wk, d_wv = d_wkv[:56], d_wkv[56:]

    own = hidden.astype(F32)
    out = (own + out_sum).astype(BF16)
    scaled = dec_gain.astype(F32) * own_grad
    d_hidden = d_out.astype(F32) + rstd * scaled - own * rstd**3 * stat
    return (out, d_hidden.astype(BF16), d_enc, d_wo, d_wk, d_wv)


def solution(mesh):
    placed = (
        P(("batch", "seq"), "nbr"),
        P(("batch", "seq"), "nbr"),
        P(("batch", "seq", "nbr"), None, None),
        P(("batch", "seq")),
        P("nbr"),
        P(),
        P("nbr", None),
        P(),
        P("seq", "nbr"),
        P("seq", "nbr"),
        P("seq", "nbr"),
        P("nbr", "seq"),
    )
    return jax.shard_map(
        body,
        mesh=mesh,
        in_specs=placed,
        out_specs=(
            P(("batch", "seq"), "nbr"),
            P(("batch", "seq"), "nbr"),
            P(("batch", "seq", "nbr"), None, None),
            P(("batch", "nbr"), "seq"),
            P(("batch", "seq"), "nbr"),
            P(("batch", "seq"), "nbr"),
        ),
        check_vma=False,
    )
```

```python
import jax
import jax.numpy as jnp
from jax import lax
from jax.experimental import pallas as pl
from jax.experimental.pallas import tpu as pltpu
from jax.sharding import PartitionSpec as P

HD = 128
CLEN = 64
NLEN = 128
KMAX = 8
F32 = jnp.float32
BF16 = jnp.bfloat16
VMEM = pl.BlockSpec(memory_space=pltpu.VMEM)
SMEM = pl.BlockSpec(memory_space=pltpu.SMEM)


def dot(a, b, dims=((1,), (0,))):
    return lax.dot_general(a, b, (dims, ((), ())), preferred_element_type=F32)


NT = ((1,), (1,))
TN = ((0,), (0,))


def shift(x, by):
    n = lax.axis_size("nbr")
    return lax.ppermute(x, "nbr", [(i, (i + by) % n) for i in range(n)])


def ring_gather(x):
    half = x.shape[0] // 2
    right = shift(x, -1)
    left = shift(x, 1)
    far_a = shift(right[:half], -1)
    far_b = shift(left[half:], 1)
    return right, far_a, far_b, left


def scattered(parts):
    return [parts[0]] + [shift(parts[r], r) for r in (2, 1, 3)]


def total(shares):
    return sum(x.astype(F32) for x in shares)


def sum_small(x):
    return x + shift(x, 1) + shift(x, 2) + shift(x, 3)


def exchange(parts):
    return lax.all_to_all(parts, "seq", split_axis=0, concat_axis=0, tiled=True)


def rms_scale(values):
    return lax.rsqrt(jnp.mean(values * values, axis=-1, keepdims=True) + 1e-06)


def cost(products, moved):
    return pl.CostEstimate(flops=2 * products, transcendentals=0, bytes_accessed=moved)


def project_kernel(n_ref, x, d, w, o):
    wq = w[:, :128].reshape(1024, 512)
    wo = w[:, 128:].reshape(1024, 512)
    tokens = x.shape[0]
    o[0, :tokens] = dot(x[...], wq).astype(BF16)
    o[0, tokens:] = dot(d[...], wo).astype(BF16)


def project(n, normed, dout, weights):
    tokens, feats = normed.shape
    return pl.pallas_call(
        project_kernel,
        grid_spec=pltpu.PrefetchScalarGridSpec(
            num_scalar_prefetch=1,
            grid=(4,),
            in_specs=[
                pl.BlockSpec((tokens, feats), lambda r, n: (0, 0)),
                pl.BlockSpec((tokens, feats), lambda r, n: (0, 0)),
                pl.BlockSpec((8, 256, 512), lambda r, n: ((n[0] + r) % 4, 0, 0)),
            ],
            out_specs=pl.BlockSpec((1, 2 * tokens, 512), lambda r, n: (r, 0, 0)),
        ),
        out_shape=jax.ShapeDtypeStruct((4, 2 * tokens, 512), BF16),
        cost_estimate=cost(2 * tokens * 4096 * 512, 12 << 20),
        compiler_params=pltpu.CompilerParams(vmem_limit_bytes=24 << 20),
        name="project",
    )(n, normed, dout, weights)


def keys_kernel(tab, e0, e1, e2, e3, wk, wv, enc, kb, vb):
    tables = ((e0, 0), (e1, 6), (e2, 12), (e3, 18))

    def pick(j, carry):
        src = tab[j]

        @pl.when(src < 0)
        def _():
            enc[j] = jnp.zeros(enc.shape[1:], BF16)

        for ref, first in tables:

            @pl.when((src >= first) & (src < first + ref.shape[0]))
            def _(ref=ref, first=first):
                enc[j] = ref[src - first]

        return carry

    lax.fori_loop(0, 2 * KMAX, pick, 0)

    def kv(c, carry):
        x = enc[pl.ds(4 * c, 4)].reshape(4 * NLEN, enc.shape[2])
        rows = pl.ds(pl.multiple_of(c * 512, 512), 512)
        kb[rows, :] = dot(x, wk[...]).astype(BF16)
        vb[rows, :] = dot(x, wv[...]).astype(BF16)
        return carry

    lax.fori_loop(0, 4, kv, 0)


def keys_values(tab, blocks, wk, wv):
    rows = 2 * KMAX * NLEN
    flat = jax.ShapeDtypeStruct((rows, wk.shape[1]), BF16)
    return pl.pallas_call(
        keys_kernel,
        in_specs=[SMEM] + [VMEM] * 6,
        out_specs=[VMEM] * 3,
        out_shape=[pltpu.HBM((2 * KMAX, NLEN, wk.shape[0]), BF16), flat, flat],
        cost_estimate=cost(2048 * 896 * 1024, 16 << 20),
        compiler_params=pltpu.CompilerParams(vmem_limit_bytes=26 << 20),
        name="keys_values",
    )(tab, *blocks, wk, wv)


def attend_kernel(tab, inv, kb, vb, q, dc, wk, wv, ctx, dq, dk, dv, out, de):
    factor = HD ** (-0.5)
    heads = q.shape[1] // HD
    keys = KMAX * NLEN
    for c in range(2):
        limit = tab[2 * KMAX + c] * NLEN
        allowed = lax.broadcasted_iota(jnp.int32, (CLEN, keys), 1) < limit
        toks = slice(c * CLEN, (c + 1) * CLEN)
        rows = slice(c * keys, (c + 1) * keys)
        for h in range(heads):
            cols = slice(h * HD, (h + 1) * HD)
            qh, dh = q[toks, cols], dc[toks, cols]
            s = jnp.where(allowed, dot(qh, kb[rows, cols], NT) * factor, -1e30)
            w = jnp.exp(s - jnp.max(s, axis=-1, keepdims=True))
            p = w / jnp.sum(w, axis=-1, keepdims=True)
            pb = p.astype(BF16)
            ctx[toks, cols] = dot(pb, vb[rows, cols]).astype(BF16)
            dp = dot(dh, vb[rows, cols], NT)
            rd = jnp.sum(p * dp, axis=-1, keepdims=True)
            ds = (p * (dp - rd) * factor).astype(BF16)
            dq[toks, cols] = dot(ds, kb[rows, cols]).astype(BF16)
            dk[rows, cols] = dot(ds, qh, TN).astype(BF16)
            dv[rows, cols] = dot(pb, dh, TN).astype(BF16)

    def grad(c, carry):
        rows = pl.ds(pl.multiple_of(c * 512, 512), 512)
        part = dot(dk[rows, :], wk[...], NT) + dot(dv[rows, :], wv[...], NT)
        de[pl.ds(4 * c, 4)] = part.astype(BF16).reshape(4, NLEN, wk.shape[0])
        return carry

    lax.fori_loop(0, 4, grad, 0)

    def place(i, carry):
        src = inv[i]

        @pl.when(src < 0)
        def _():
            out[i] = jnp.zeros(out.shape[1:], BF16)

        @pl.when(src >= 0)
        def _():
            out[i] = de[src]

        return carry

    lax.fori_loop(0, out.shape[0], place, 0)


def attend(tab, inv, kb, vb, q, dc, wk, wv):
    width = wk.shape[0]
    same = jax.ShapeDtypeStruct(q.shape, BF16)
    flat = pltpu.HBM(kb.shape, BF16)
    return pl.pallas_call(
        attend_kernel,
        in_specs=[SMEM, SMEM] + [VMEM] * 6,
        out_specs=[VMEM] * 5,
        out_shape=[same, same, flat, flat, pltpu.HBM((inv.shape[0], NLEN, width), BF16)],
        scratch_shapes=[pltpu.VMEM((2 * KMAX, NLEN, width), BF16)],
        cost_estimate=cost(2048 * 896 * 1024, 40 << 20),
        compiler_params=pltpu.CompilerParams(vmem_limit_bytes=34 << 20),
        name="attend",
    )(tab, inv, kb, vb, q, dc, wk, wv)


def finish_kernel(n_ref, x, hid, dout, gain, rstd, stat, w, out, dhid, oa, na):
    step = pl.program_id(0)
    tokens = hid.shape[0]
    wq = w[:, :128].reshape(1024, 512)
    wo = w[:, 128:].reshape(1024, 512)
    o_part = dot(x[0, :tokens], wo, NT)
    n_part = dot(x[0, tokens : 2 * tokens], wq, NT)

    @pl.when(step == 0)
    def _():
        oa[...] = o_part
        na[...] = n_part

    @pl.when((step > 0) & (step < 3))
    def _():
        oa[...] += o_part
        na[...] += n_part

    @pl.when(step == 3)
    def _():
        own = hid[...].astype(F32)
        scale = rstd[...]
        out[...] = (own + (oa[...] + o_part)).astype(BF16)
        scaled = gain[...].astype(F32) * (na[...] + n_part)
        grad = dout[...].astype(F32) + scale * scaled - own * (scale * scale * scale) * stat[...]
        dhid[...] = grad.astype(BF16)


def finish(n, x, hidden, dout, gain, rstd, stat, weights):
    tokens, feats = hidden.shape
    whole = pl.BlockSpec((tokens, feats), lambda r, n: (0, 0))
    column = pl.BlockSpec((tokens, 1), lambda r, n: (0, 0))
    return pl.pallas_call(
        finish_kernel,
        grid_spec=pltpu.PrefetchScalarGridSpec(
            num_scalar_prefetch=1,
            grid=(4,),
            in_specs=[
                pl.BlockSpec((1, x.shape[1], 512), lambda r, n: (r, 0, 0)),
                whole,
                whole,
                pl.BlockSpec((1, feats), lambda r, n: (0, 0)),
                column,
                column,
                pl.BlockSpec((8, 256, 512), lambda r, n: ((n[0] + r) % 4, 0, 0)),
            ],
            out_specs=[whole, whole],
            scratch_shapes=[pltpu.VMEM((tokens, feats), F32)] * 2,
        ),
        out_shape=[jax.ShapeDtypeStruct((tokens, feats), BF16)] * 2,
        cost_estimate=cost(2 * tokens * 4096 * 512, 12 << 20),
        compiler_params=pltpu.CompilerParams(vmem_limit_bytes=24 << 20),
        name="finish",
    )(n, x, hidden, dout, gain[None], rstd, stat, weights)


def outer_kernel(at, d, ctx, a0, a1, a2, a3, b0, b1, b2, b3):
    n, x, z = at[0], at[1], at[2]
    upper, lower = (a0, a1, a2, a3), (b0, b1, b2, b3)
    half = a0.shape[1]
    for i in range(4):
        block = lax.rem(x + i + 4 - n, 4)
        for j in range(4):
            first = pl.multiple_of(lax.rem(z + j, 4) * 2 * half, 2 * half)
            part = dot(d[block, :, pl.ds(first, 2 * half)], ctx[...], TN).astype(BF16)
            upper[i][j] = part[:half]
            lower[j][i] = part[half:]


def outer(at, dout, ctx):
    share = jax.ShapeDtypeStruct((4, 128, ctx.shape[1]), BF16)
    return pl.pallas_call(
        outer_kernel,
        in_specs=[SMEM, VMEM, VMEM],
        out_specs=[VMEM] * 8,
        out_shape=[share] * 8,
        cost_estimate=cost(ctx.shape[0] * 4096 * 512, 6 << 20),
        compiler_params=pltpu.CompilerParams(vmem_limit_bytes=24 << 20),
        name="outer",
    )(at, dout, ctx)


def along_x(share, by):
    return lax.ppermute(share, "seq", [(i, (i // 4 + by) % 4 * 4 + i % 4) for i in range(16)])


def along_z(share, by):
    return lax.ppermute(share, "seq", [(i, i // 4 * 4 + (i + by) % 4) for i in range(16)])


def slot_tables(slot_span, n):
    slots = slot_span.shape[0]
    ids = jnp.arange(slots, dtype=jnp.int32)
    before = ids[None, :] < ids[:, None]
    same = slot_span[None, :] == slot_span[:, None]
    rank = jnp.sum(same & before, axis=1, dtype=jnp.int32)
    where = jnp.where(slot_span >= 0, slot_span * KMAX + rank, -1).astype(jnp.int32)
    spot = jnp.arange(2 * KMAX, dtype=jnp.int32)
    hit = where[None, :] == spot[:, None]
    relative = (ids + slots - 6 * n) % slots
    source = jnp.sum(jnp.where(hit, relative[None, :] + 1, 0), axis=1, dtype=jnp.int32) - 1
    counts = jnp.sum(slot_span[None, :] == jnp.arange(2)[:, None], axis=1, dtype=jnp.int32)
    return jnp.concatenate([source, counts]), where


def body(hidden, d_out, nbr_emb, slot_span, dec_gain, enc_gain, w_cond, w_enc, w_q, w_k, w_v, w_o):
    n = lax.axis_index("nbr")
    b = lax.axis_index("batch")
    n1 = n.astype(jnp.int32).reshape(1)
    tokens, feats = hidden.shape
    spans = tokens // CLEN

    q_half = lax.dynamic_slice_in_dim(w_q, b * 128, 128, axis=0)
    o_half = lax.dynamic_slice_in_dim(w_o, b * 128, 128, axis=1).T
    kv_half = jnp.where(b == 0, w_k, w_v)
    swap = [
        ((4 * i + j) * 4 + k, (4 * k + j) * 4 + i)
        for i in range(4)
        for j in range(4)
        for k in range(4)
    ]
    qo_half = lax.ppermute(jnp.concatenate([q_half, o_half], axis=0), ("seq", "nbr"), swap)
    weights = lax.all_gather(
        jnp.concatenate([qo_half, kv_half], axis=0), ("seq", "batch"), axis=0
    )

    hf = hidden.astype(F32)
    pooled = jnp.mean(hf.reshape(spans, CLEN, feats), axis=1).astype(BF16)
    squares = jnp.sum(hf * hf, axis=-1)
    length = lax.axis_size("seq")
    carried = lax.ppermute(
        pooled[spans - 1 :], "seq", [(i, i + 1) for i in range(length - 1)]
    )
    previous = jnp.concatenate([carried, pooled[: spans - 1]], axis=0)
    width = nbr_emb.shape[2]
    small = jnp.concatenate(
        [
            jnp.dot(previous, w_cond, preferred_element_type=F32),
            jnp.pad(squares, (0, width - tokens))[None],
        ],
        axis=0,
    )
    small = sum_small(small)
    condition = small[:spans]
    rstd = lax.rsqrt(small[spans, :tokens] / (4 * feats) + 1e-06)[:, None]
    normed = (hf * rstd * dec_gain.astype(F32)).astype(BF16)

    nbr_emb = lax.optimization_barrier((nbr_emb, condition))[0]
    e1, e2a, e2b, e3 = ring_gather(nbr_emb)
    later = lax.optimization_barrier((d_out, e1, e3))[0]
    d2, d1, d3 = (shift(later, r) for r in (2, -1, 1))
    dout_rel = jnp.stack([d_out, d1, d2, d3])

    tab, inv = slot_tables(slot_span, n)
    rel_span = jnp.roll(slot_span.reshape(4, 6), -n, axis=0).reshape(-1)

    def encode(block, first):
        own = lax.slice_in_dim(rel_span, first, first + block.shape[0])
        own = own[:, None, None]
        cond = jnp.where(own == 0, condition[0], jnp.where(own == 1, condition[1], 0.0))
        x = block.astype(F32) + cond
        enc_normed = (x * rms_scale(x) * enc_gain.astype(F32)).astype(BF16)
        width = x.shape[2]
        mixed = jnp.dot(
            enc_normed.reshape(-1, width), w_enc, preferred_element_type=F32
        ).reshape(x.shape)
        return (x + jax.nn.silu(mixed)).astype(BF16)


    pairs = weights.reshape(16, 2, 312, 512)
    weights = pltpu.with_memory_space_constraint(weights, pltpu.HBM)
    wk = pairs[:, 0, 256:].reshape(-1, 512)
    wv = pairs[:, 1, 256:].reshape(-1, 512)

    normed, dout_rel = lax.optimization_barrier((normed, dout_rel))
    shares = scattered(project(n1, normed, d_out, weights))
    both = total(shares).astype(BF16)
    query, d_ctx = both[:tokens], both[tokens:]
    e2 = jnp.concatenate([e2a, e2b], axis=0)
    encoded = [encode(nbr_emb, 0), encode(e1, 6), encode(e2, 12), encode(e3, 18)]
    enc, keys, values = keys_values(tab, encoded, wk, wv)
    ctx, d_query, d_key, d_value, parts = attend(
        tab, inv, keys, values, query, d_ctx, wk, wv
    )
    d_enc = lax.psum_scatter(parts, "nbr", scatter_dimension=0, tiled=True)

    inner = jnp.sum(d_query.astype(F32) * query.astype(F32), axis=-1).astype(BF16)
    more = jnp.broadcast_to(jnp.pad(inner, (0, ctx.shape[1] - tokens))[None], (16, ctx.shape[1]))
    local = jnp.concatenate([ctx, d_query, more], axis=0)
    heads = jnp.stack([local, shift(local, -1), shift(local, 2), shift(local, 1)])
    stat = jnp.sum(heads[:, 2 * tokens, :tokens].astype(F32), axis=0)[:, None]
    stat = stat / (rstd * (4 * feats))
    out, d_hidden = finish(n1, heads, hidden, d_out, dec_gain, rstd, stat, weights)

    place = lax.axis_index("seq").astype(jnp.int32)
    at = jnp.stack([n.astype(jnp.int32), place // 4, place % 4])
    d_wo_parts = outer(at, dout_rel, ctx)
    upper = [along_x(d_wo_parts[i], i) for i in (2, 1, 3)]
    lower = [along_z(d_wo_parts[4 + i], i) for i in (2, 1, 3)]
    upper = total([d_wo_parts[0]] + upper).astype(BF16)
    lower = total([d_wo_parts[4]] + lower).astype(BF16)
    upper = total([upper[0]] + [along_z(upper[i], i) for i in (2, 1, 3)])
    lower = total([lower[0]] + [along_x(lower[i], i) for i in (2, 1, 3)])
    d_wo = jnp.concatenate([upper, lower], axis=0).T

    rows = enc.reshape(-1, enc.shape[2])
    d_wk_part = dot(rows, d_key, TN).astype(BF16).reshape(16, -1, 512)
    d_wv_part = dot(rows, d_value, TN).astype(BF16).reshape(16, -1, 512)
    d_wkv_parts = jnp.concatenate([d_wk_part, d_wv_part], axis=1)
    d_wkv = jnp.sum(exchange(d_wkv_parts).astype(F32), axis=0)
    d_wk, d_wv = d_wkv[:56], d_wkv[56:]

    return (out, d_hidden, d_enc, d_wo, d_wk, d_wv)


def solution(mesh):
    placed = (
        P(("batch", "seq"), "nbr"),
        P(("batch", "seq"), "nbr"),
        P(("batch", "seq", "nbr"), None, None),
        P(("batch", "seq")),
        P("nbr"),
        P(),
        P("nbr", None),
        P(),
        P("seq", "nbr"),
        P("seq", "nbr"),
        P("seq", "nbr"),
        P("nbr", "seq"),
    )
    return jax.shard_map(
        body,
        mesh=mesh,
        in_specs=placed,
        out_specs=(
            P(("batch", "seq"), "nbr"),
            P(("batch", "seq"), "nbr"),
            P(("batch", "seq", "nbr"), None, None),
            P(("batch", "nbr"), "seq"),
            P(("batch", "seq"), "nbr"),
            P(("batch", "seq"), "nbr"),
        ),
        check_vma=False,
    )
```

```python
import jax
import jax.numpy as jnp
from jax import lax
from jax.experimental import pallas as pl
from jax.experimental.pallas import tpu as pltpu
from jax.sharding import PartitionSpec as P

HD = 128
CLEN = 64
NLEN = 128
KMAX = 8
F32 = jnp.float32
BF16 = jnp.bfloat16
VMEM = pl.BlockSpec(memory_space=pltpu.VMEM)
SMEM = pl.BlockSpec(memory_space=pltpu.SMEM)


def dot(a, b, dims=((1,), (0,))):
    return lax.dot_general(a, b, (dims, ((), ())), preferred_element_type=F32)


NT = ((1,), (1,))
TN = ((0,), (0,))


def shift(x, by):
    n = lax.axis_size("nbr")
    return lax.ppermute(x, "nbr", [(i, (i + by) % n) for i in range(n)])


def ring_gather(x):
    half = x.shape[0] // 2
    right = shift(x, -1)
    left = shift(x, 1)
    far_a = shift(right[:half], -1)
    far_b = shift(left[half:], 1)
    return right, far_a, far_b, left


def scattered(parts):
    return [parts[0]] + [shift(parts[r], r) for r in (2, 1, 3)]


def total(shares):
    return sum(x.astype(F32) for x in shares)


def sum_small(x):
    return x + shift(x, 1) + shift(x, 2) + shift(x, 3)


def exchange(parts):
    return lax.all_to_all(parts, "seq", split_axis=0, concat_axis=0, tiled=True)


def rms_scale(values):
    return lax.rsqrt(jnp.mean(values * values, axis=-1, keepdims=True) + 1e-06)


def cost(products, moved):
    return pl.CostEstimate(flops=2 * products, transcendentals=0, bytes_accessed=moved)


def project_kernel(n_ref, x, d, w, o):
    tokens = x.shape[0]
    q = jnp.zeros((tokens, 512), F32)
    dc = jnp.zeros((tokens, 512), F32)
    for s in range(4):
        cols = slice(256 * s, 256 * s + 256)
        q += dot(x[:, cols], w[2 * s])
        dc += dot(d[:, cols], w[2 * s + 1])
    o[0, :tokens] = q.astype(BF16)
    o[0, tokens:] = dc.astype(BF16)


def project(n, normed, dout, weights):
    tokens, feats = normed.shape
    return pl.pallas_call(
        project_kernel,
        grid_spec=pltpu.PrefetchScalarGridSpec(
            num_scalar_prefetch=1,
            grid=(4,),
            in_specs=[
                pl.BlockSpec((tokens, feats), lambda r, n: (0, 0)),
                pl.BlockSpec((tokens, feats), lambda r, n: (0, 0)),
                pl.BlockSpec((8, 256, 512), lambda r, n: ((2 * n[0] + r) % 4, 0, 0)),
            ],
            out_specs=pl.BlockSpec((1, 2 * tokens, 512), lambda r, n: (r, 0, 0)),
        ),
        out_shape=jax.ShapeDtypeStruct((4, 2 * tokens, 512), BF16),
        cost_estimate=cost(2 * tokens * 4096 * 512, 12 << 20),
        compiler_params=pltpu.CompilerParams(vmem_limit_bytes=24 << 20),
        name="project",
    )(n, normed, dout, weights)


def keys_kernel(tab, e0, e1, e2, e3, wk, wv, enc, kb, vb):
    tables = ((e0, 0), (e1, 6), (e2, 12), (e3, 18))

    def pick(j, carry):
        src = tab[j]

        @pl.when(src < 0)
        def _():
            enc[j] = jnp.zeros(enc.shape[1:], BF16)

        for ref, first in tables:

            @pl.when((src >= first) & (src < first + ref.shape[0]))
            def _(ref=ref, first=first):
                enc[j] = ref[src - first]

        return carry

    lax.fori_loop(0, 2 * KMAX, pick, 0)

    def kv(c, carry):
        x = enc[pl.ds(4 * c, 4)].reshape(4 * NLEN, enc.shape[2])
        rows = pl.ds(pl.multiple_of(c * 512, 512), 512)
        kb[rows, :] = dot(x, wk[...]).astype(BF16)
        vb[rows, :] = dot(x, wv[...]).astype(BF16)
        return carry

    lax.fori_loop(0, 4, kv, 0)


def keys_values(tab, blocks, wk, wv):
    rows = 2 * KMAX * NLEN
    flat = jax.ShapeDtypeStruct((rows, wk.shape[1]), BF16)
    return pl.pallas_call(
        keys_kernel,
        in_specs=[SMEM] + [VMEM] * 6,
        out_specs=[VMEM] * 3,
        out_shape=[pltpu.HBM((2 * KMAX, NLEN, wk.shape[0]), BF16), flat, flat],
        cost_estimate=cost(2048 * 896 * 1024, 16 << 20),
        compiler_params=pltpu.CompilerParams(vmem_limit_bytes=26 << 20),
        name="keys_values",
    )(tab, *blocks, wk, wv)


def attend_kernel(tab, inv, kb, vb, q, dc, wk, wv, ctx, dq, dk, dv, out, de):
    factor = HD ** (-0.5)
    heads = q.shape[1] // HD
    keys = KMAX * NLEN
    for c in range(2):
        limit = tab[2 * KMAX + c] * NLEN
        allowed = lax.broadcasted_iota(jnp.int32, (CLEN, keys), 1) < limit
        toks = slice(c * CLEN, (c + 1) * CLEN)
        rows = slice(c * keys, (c + 1) * keys)
        for h in range(heads):
            cols = slice(h * HD, (h + 1) * HD)
            qh, dh = q[toks, cols], dc[toks, cols]
            s = jnp.where(allowed, dot(qh, kb[rows, cols], NT) * factor, -1e30)
            w = jnp.exp(s - jnp.max(s, axis=-1, keepdims=True))
            p = w / jnp.sum(w, axis=-1, keepdims=True)
            pb = p.astype(BF16)
            ctx[toks, cols] = dot(pb, vb[rows, cols]).astype(BF16)
            dp = dot(dh, vb[rows, cols], NT)
            rd = jnp.sum(p * dp, axis=-1, keepdims=True)
            ds = (p * (dp - rd) * factor).astype(BF16)
            dq[toks, cols] = dot(ds, kb[rows, cols]).astype(BF16)
            dk[rows, cols] = dot(ds, qh, TN).astype(BF16)
            dv[rows, cols] = dot(pb, dh, TN).astype(BF16)

    def grad(c, carry):
        rows = pl.ds(pl.multiple_of(c * 512, 512), 512)
        part = dot(dk[rows, :], wk[...], NT) + dot(dv[rows, :], wv[...], NT)
        de[pl.ds(4 * c, 4)] = part.astype(BF16).reshape(4, NLEN, wk.shape[0])
        return carry

    lax.fori_loop(0, 4, grad, 0)

    def place(i, carry):
        src = inv[i]

        @pl.when(src < 0)
        def _():
            out[i] = jnp.zeros(out.shape[1:], BF16)

        @pl.when(src >= 0)
        def _():
            out[i] = de[src]

        return carry

    lax.fori_loop(0, out.shape[0], place, 0)


def attend(tab, inv, kb, vb, q, dc, wk, wv):
    width = wk.shape[0]
    same = jax.ShapeDtypeStruct(q.shape, BF16)
    flat = pltpu.HBM(kb.shape, BF16)
    return pl.pallas_call(
        attend_kernel,
        in_specs=[SMEM, SMEM] + [VMEM] * 6,
        out_specs=[VMEM] * 5,
        out_shape=[same, same, flat, flat, pltpu.HBM((inv.shape[0], NLEN, width), BF16)],
        scratch_shapes=[pltpu.VMEM((2 * KMAX, NLEN, width), BF16)],
        cost_estimate=cost(2048 * 896 * 1024, 40 << 20),
        compiler_params=pltpu.CompilerParams(vmem_limit_bytes=34 << 20),
        name="attend",
    )(tab, inv, kb, vb, q, dc, wk, wv)


def finish_kernel(n_ref, x, hid, dout, gain, rstd, stat, w, out, dhid, oa, na):
    step = pl.program_id(0)
    tokens = hid.shape[0]
    o_part = jnp.concatenate([dot(x[0, :tokens], w[2 * s + 1], NT) for s in range(4)], axis=1)
    dq = x[0, tokens : 2 * tokens]
    n_part = jnp.concatenate([dot(dq, w[2 * s], NT) for s in range(4)], axis=1)

    @pl.when(step == 0)
    def _():
        oa[...] = o_part
        na[...] = n_part

    @pl.when((step > 0) & (step < 3))
    def _():
        oa[...] += o_part
        na[...] += n_part

    @pl.when(step == 3)
    def _():
        own = hid[...].astype(F32)
        scale = rstd[...]
        out[...] = (own + (oa[...] + o_part)).astype(BF16)
        scaled = gain[...].astype(F32) * (na[...] + n_part)
        grad = dout[...].astype(F32) + scale * scaled - own * (scale * scale * scale) * stat[...]
        dhid[...] = grad.astype(BF16)


def finish(n, x, hidden, dout, gain, rstd, stat, weights):
    tokens, feats = hidden.shape
    whole = pl.BlockSpec((tokens, feats), lambda r, n: (0, 0))
    column = pl.BlockSpec((tokens, 1), lambda r, n: (0, 0))
    return pl.pallas_call(
        finish_kernel,
        grid_spec=pltpu.PrefetchScalarGridSpec(
            num_scalar_prefetch=1,
            grid=(4,),
            in_specs=[
                pl.BlockSpec((1, x.shape[1], 512), lambda r, n: (r, 0, 0)),
                whole,
                whole,
                pl.BlockSpec((1, feats), lambda r, n: (0, 0)),
                column,
                column,
                pl.BlockSpec((8, 256, 512), lambda r, n: ((2 * n[0] + r) % 4, 0, 0)),
            ],
            out_specs=[whole, whole],
            scratch_shapes=[pltpu.VMEM((tokens, feats), F32)] * 2,
        ),
        out_shape=[jax.ShapeDtypeStruct((tokens, feats), BF16)] * 2,
        cost_estimate=cost(2 * tokens * 4096 * 512, 12 << 20),
        compiler_params=pltpu.CompilerParams(vmem_limit_bytes=24 << 20),
        name="finish",
    )(n, x, hidden, dout, gain[None], rstd, stat, weights)


def outer_kernel(n_ref, d, ctx, o):
    for s in range(4):
        o[s] = dot(d[0, :, 256 * s : 256 * s + 256], ctx[...], TN).astype(BF16)


def outer(n, dout, ctx):
    tokens = ctx.shape[0]
    return pl.pallas_call(
        outer_kernel,
        grid_spec=pltpu.PrefetchScalarGridSpec(
            num_scalar_prefetch=1,
            grid=(4,),
            in_specs=[
                pl.BlockSpec((1, tokens, 1024), lambda r, n: (r, 0, 0)),
                pl.BlockSpec((tokens, 512), lambda r, n: (0, 0)),
            ],
            out_specs=pl.BlockSpec((4, 256, 512), lambda r, n: ((n[0] + r) % 4, 0, 0)),
        ),
        out_shape=pltpu.HBM((16, 256, 512), BF16),
        cost_estimate=cost(tokens * 4096 * 512, 6 << 20),
        compiler_params=pltpu.CompilerParams(vmem_limit_bytes=16 << 20),
        name="outer",
    )(n, dout, ctx)


def along_x(share, by):
    return lax.ppermute(share, "seq", [(i, (i // 4 + by) % 4 * 4 + i % 4) for i in range(16)])


def along_z(share, by):
    return lax.ppermute(share, "seq", [(i, i // 4 * 4 + (i + by) % 4) for i in range(16)])


def slot_tables(slot_span, n):
    slots = slot_span.shape[0]
    ids = jnp.arange(slots, dtype=jnp.int32)
    before = ids[None, :] < ids[:, None]
    same = slot_span[None, :] == slot_span[:, None]
    rank = jnp.sum(same & before, axis=1, dtype=jnp.int32)
    where = jnp.where(slot_span >= 0, slot_span * KMAX + rank, -1).astype(jnp.int32)
    spot = jnp.arange(2 * KMAX, dtype=jnp.int32)
    hit = where[None, :] == spot[:, None]
    relative = (ids + slots - 6 * n) % slots
    source = jnp.sum(jnp.where(hit, relative[None, :] + 1, 0), axis=1, dtype=jnp.int32) - 1
    counts = jnp.sum(slot_span[None, :] == jnp.arange(2)[:, None], axis=1, dtype=jnp.int32)
    return jnp.concatenate([source, counts]), where


def body(hidden, d_out, nbr_emb, slot_span, dec_gain, enc_gain, w_cond, w_enc, w_q, w_k, w_v, w_o):
    n = lax.axis_index("nbr")
    b = lax.axis_index("batch")
    n1 = n.astype(jnp.int32).reshape(1)
    tokens, feats = hidden.shape
    spans = tokens // CLEN

    kv_half = jnp.where(b == 0, w_k, w_v)
    swap = [
        ((4 * i + j) * 4 + k, ((i + k) % 4 * 4 + j) * 4 + i)
        for i in range(4)
        for j in range(4)
        for k in range(4)
    ]
    qo_half = lax.ppermute(jnp.where(b == 0, w_q, w_o.T), ("seq", "nbr"), swap)
    weights = lax.all_gather(
        jnp.concatenate([qo_half, kv_half], axis=0), ("seq", "batch"), axis=0
    )

    hf = hidden.astype(F32)
    pooled = jnp.mean(hf.reshape(spans, CLEN, feats), axis=1).astype(BF16)
    squares = jnp.sum(hf * hf, axis=-1)
    length = lax.axis_size("seq")
    carried = lax.ppermute(
        pooled[spans - 1 :], "seq", [(i, i + 1) for i in range(length - 1)]
    )
    previous = jnp.concatenate([carried, pooled[: spans - 1]], axis=0)
    width = nbr_emb.shape[2]
    small = jnp.concatenate(
        [
            jnp.dot(previous, w_cond, preferred_element_type=F32),
            jnp.pad(squares, (0, width - tokens))[None],
        ],
        axis=0,
    )
    small = sum_small(small)
    condition = small[:spans]
    rstd = lax.rsqrt(small[spans, :tokens] / (4 * feats) + 1e-06)[:, None]
    normed = (hf * rstd * dec_gain.astype(F32)).astype(BF16)

    nbr_emb = lax.optimization_barrier((nbr_emb, condition))[0]
    e1, e2a, e2b, e3 = ring_gather(nbr_emb)
    later = lax.optimization_barrier((d_out, e1, e3))[0]
    d2, d1, d3 = (shift(later, r) for r in (2, -1, 1))
    dout_rel = jnp.stack([d_out, d1, d2, d3])

    tab, inv = slot_tables(slot_span, n)
    rel_span = jnp.roll(slot_span.reshape(4, 6), -n, axis=0).reshape(-1)

    def encode(block, first):
        own = lax.slice_in_dim(rel_span, first, first + block.shape[0])
        own = own[:, None, None]
        cond = jnp.where(own == 0, condition[0], jnp.where(own == 1, condition[1], 0.0))
        x = block.astype(F32) + cond
        enc_normed = (x * rms_scale(x) * enc_gain.astype(F32)).astype(BF16)
        width = x.shape[2]
        mixed = jnp.dot(
            enc_normed.reshape(-1, width), w_enc, preferred_element_type=F32
        ).reshape(x.shape)
        return (x + jax.nn.silu(mixed)).astype(BF16)


    pairs = weights.reshape(16, 2, 312, 512)
    weights = pltpu.with_memory_space_constraint(weights, pltpu.HBM)
    wk = pairs[:, 0, 256:].reshape(-1, 512)
    wv = pairs[:, 1, 256:].reshape(-1, 512)

    normed, dout_rel = lax.optimization_barrier((normed, dout_rel))
    shares = scattered(project(n1, normed, d_out, weights))
    both = total(shares).astype(BF16)
    query, d_ctx = both[:tokens], both[tokens:]
    e2 = jnp.concatenate([e2a, e2b], axis=0)
    encoded = [encode(nbr_emb, 0), encode(e1, 6), encode(e2, 12), encode(e3, 18)]
    enc, keys, values = keys_values(tab, encoded, wk, wv)
    ctx, d_query, d_key, d_value, parts = attend(
        tab, inv, keys, values, query, d_ctx, wk, wv
    )
    d_enc = lax.psum_scatter(parts, "nbr", scatter_dimension=0, tiled=True)

    inner = jnp.sum(d_query.astype(F32) * query.astype(F32), axis=-1).astype(BF16)
    more = jnp.broadcast_to(jnp.pad(inner, (0, ctx.shape[1] - tokens))[None], (16, ctx.shape[1]))
    local = jnp.concatenate([ctx, d_query, more], axis=0)
    heads = jnp.stack([local, shift(local, -1), shift(local, 2), shift(local, 1)])
    stat = jnp.sum(heads[:, 2 * tokens, :tokens].astype(F32), axis=0)[:, None]
    stat = stat / (rstd * (4 * feats))
    out, d_hidden = finish(n1, heads, hidden, d_out, dec_gain, rstd, stat, weights)

    d_wo = jnp.sum(exchange(outer(n1, dout_rel, ctx)).astype(F32), axis=0).T

    rows = enc.reshape(-1, enc.shape[2])
    place = lax.axis_index("seq")
    px, pz = place // 4, place % 4

    def block(parts, i, dim):
        return lax.dynamic_index_in_dim(parts, i % 4, dim, keepdims=False)

    wk_parts = dot(rows, d_key, TN).astype(BF16).reshape(4, 4, -1, 512)
    wv_parts = dot(rows, d_value, TN).astype(BF16).reshape(4, 4, -1, 512)
    wk_sum = [block(wk_parts, px, 0)] + [along_x(block(wk_parts, px + i, 0), i) for i in (2, 1, 3)]
    wv_sum = [block(wv_parts, pz, 1)] + [along_z(block(wv_parts, pz + i, 1), i) for i in (2, 1, 3)]
    wk_sum, wv_sum = total(wk_sum).astype(BF16), total(wv_sum).astype(BF16)
    d_wk = [block(wk_sum, pz, 0)] + [along_z(block(wk_sum, pz + i, 0), i) for i in (2, 1, 3)]
    d_wv = [block(wv_sum, px, 0)] + [along_x(block(wv_sum, px + i, 0), i) for i in (2, 1, 3)]
    d_wk, d_wv = total(d_wk), total(d_wv)

    return (out, d_hidden, d_enc, d_wo, d_wk, d_wv)


def solution(mesh):
    placed = (
        P(("batch", "seq"), "nbr"),
        P(("batch", "seq"), "nbr"),
        P(("batch", "seq", "nbr"), None, None),
        P(("batch", "seq")),
        P("nbr"),
        P(),
        P("nbr", None),
        P(),
        P("seq", "nbr"),
        P("seq", "nbr"),
        P("seq", "nbr"),
        P("nbr", "seq"),
    )
    return jax.shard_map(
        body,
        mesh=mesh,
        in_specs=placed,
        out_specs=(
            P(("batch", "seq"), "nbr"),
            P(("batch", "seq"), "nbr"),
            P(("batch", "seq", "nbr"), None, None),
            P(("batch", "nbr"), "seq"),
            P(("batch", "seq"), "nbr"),
            P(("batch", "seq"), "nbr"),
        ),
        check_vma=False,
    )
```

```python
import jax
import jax.numpy as jnp
from jax import lax
from jax.experimental import pallas as pl
from jax.experimental.pallas import tpu as pltpu
from jax.sharding import PartitionSpec as P

HD = 128
CLEN = 64
NLEN = 128
KMAX = 8
F32 = jnp.float32
BF16 = jnp.bfloat16
VMEM = pl.BlockSpec(memory_space=pltpu.VMEM)
SMEM = pl.BlockSpec(memory_space=pltpu.SMEM)


def dot(a, b, dims=((1,), (0,))):
    return lax.dot_general(a, b, (dims, ((), ())), preferred_element_type=F32)


NT = ((1,), (1,))
TN = ((0,), (0,))


def shift(x, by):
    n = lax.axis_size("nbr")
    return lax.ppermute(x, "nbr", [(i, (i + by) % n) for i in range(n)])


def ring_gather(x):
    half = x.shape[0] // 2
    right = shift(x, -1)
    left = shift(x, 1)
    far_a = shift(right[:half], -1)
    far_b = shift(left[half:], 1)
    return right, far_a, far_b, left


def scattered(parts):
    return [parts[0]] + [shift(parts[r], r) for r in (2, 1, 3)]


def total(shares):
    return sum(x.astype(F32) for x in shares)


def sum_small(x):
    return x + shift(x, 1) + shift(x, 2) + shift(x, 3)


def rms_scale(values):
    return lax.rsqrt(jnp.mean(values * values, axis=-1, keepdims=True) + 1e-06)


def cost(products, moved):
    return pl.CostEstimate(flops=2 * products, transcendentals=0, bytes_accessed=moved)


def project_kernel(n_ref, x, d, wq, wo, o):
    tokens = x.shape[0]
    q = jnp.zeros((tokens, 512), F32)
    dc = jnp.zeros((tokens, 512), F32)
    for s in range(4):
        cols = slice(256 * s, 256 * s + 256)
        q += dot(x[:, cols], wq[s, 0])
        dc += dot(d[:, cols], wo[s, 0])
    o[0, :tokens] = q.astype(BF16)
    o[0, tokens:] = dc.astype(BF16)


def project(n, normed, dout, weights):
    tokens, feats = normed.shape
    return pl.pallas_call(
        project_kernel,
        grid_spec=pltpu.PrefetchScalarGridSpec(
            num_scalar_prefetch=1,
            grid=(4,),
            in_specs=[
                pl.BlockSpec((tokens, feats), lambda r, n: (0, 0)),
                pl.BlockSpec((tokens, feats), lambda r, n: (0, 0)),
                pl.BlockSpec((4, 1, 256, 512), lambda r, n: ((2 * n[0] + r) % 4, 0, 0, 0)),
                pl.BlockSpec((4, 1, 256, 512), lambda r, n: ((4 - r) % 4, 1, 0, 0)),
            ],
            out_specs=pl.BlockSpec((1, 2 * tokens, 512), lambda r, n: (r, 0, 0)),
        ),
        out_shape=jax.ShapeDtypeStruct((4, 2 * tokens, 512), BF16),
        cost_estimate=cost(2 * tokens * 4096 * 512, 12 << 20),
        compiler_params=pltpu.CompilerParams(vmem_limit_bytes=24 << 20),
        name="project",
    )(n, normed, dout, weights, weights)


def keys_kernel(tab, e0, e1, e2, e3, wk, wv, enc, kb, vb):
    tables = ((e0, 0), (e1, 6), (e2, 12), (e3, 18))

    def pick(j, carry):
        src = tab[j]

        @pl.when(src < 0)
        def _():
            enc[j] = jnp.zeros(enc.shape[1:], BF16)

        for ref, first in tables:

            @pl.when((src >= first) & (src < first + ref.shape[0]))
            def _(ref=ref, first=first):
                enc[j] = ref[src - first]

        return carry

    lax.fori_loop(0, 2 * KMAX, pick, 0)

    def kv(c, carry):
        x = enc[pl.ds(4 * c, 4)].reshape(4 * NLEN, enc.shape[2])
        rows = pl.ds(pl.multiple_of(c * 512, 512), 512)
        kb[rows, :] = dot(x, wk[...]).astype(BF16)
        vb[rows, :] = dot(x, wv[...]).astype(BF16)
        return carry

    lax.fori_loop(0, 4, kv, 0)


def keys_values(tab, blocks, wk, wv):
    rows = 2 * KMAX * NLEN
    flat = jax.ShapeDtypeStruct((rows, wk.shape[1]), BF16)
    return pl.pallas_call(
        keys_kernel,
        in_specs=[SMEM] + [VMEM] * 6,
        out_specs=[VMEM] * 3,
        out_shape=[pltpu.HBM((2 * KMAX, NLEN, wk.shape[0]), BF16), flat, flat],
        cost_estimate=cost(2048 * 896 * 1024, 16 << 20),
        compiler_params=pltpu.CompilerParams(vmem_limit_bytes=26 << 20),
        name="keys_values",
    )(tab, *blocks, wk, wv)


def attend_kernel(tab, inv, kb, vb, q, dc, wk, wv, ctx, dq, dk, dv, out, de):
    factor = HD ** (-0.5)
    heads = q.shape[1] // HD
    keys = KMAX * NLEN
    for c in range(2):
        limit = tab[2 * KMAX + c] * NLEN
        allowed = lax.broadcasted_iota(jnp.int32, (CLEN, keys), 1) < limit
        toks = slice(c * CLEN, (c + 1) * CLEN)
        rows = slice(c * keys, (c + 1) * keys)
        for h in range(heads):
            cols = slice(h * HD, (h + 1) * HD)
            qh, dh = q[toks, cols], dc[toks, cols]
            s = jnp.where(allowed, dot(qh, kb[rows, cols], NT) * factor, -1e30)
            w = jnp.exp(s - jnp.max(s, axis=-1, keepdims=True))
            p = w / jnp.sum(w, axis=-1, keepdims=True)
            pb = p.astype(BF16)
            ctx[toks, cols] = dot(pb, vb[rows, cols]).astype(BF16)
            dp = dot(dh, vb[rows, cols], NT)
            rd = jnp.sum(p * dp, axis=-1, keepdims=True)
            ds = (p * (dp - rd) * factor).astype(BF16)
            dq[toks, cols] = dot(ds, kb[rows, cols]).astype(BF16)
            dk[rows, cols] = dot(ds, qh, TN).astype(BF16)
            dv[rows, cols] = dot(pb, dh, TN).astype(BF16)

    def grad(c, carry):
        rows = pl.ds(pl.multiple_of(c * 512, 512), 512)
        part = dot(dk[rows, :], wk[...], NT) + dot(dv[rows, :], wv[...], NT)
        de[pl.ds(4 * c, 4)] = part.astype(BF16).reshape(4, NLEN, wk.shape[0])
        return carry

    lax.fori_loop(0, 4, grad, 0)

    def place(i, carry):
        src = inv[i]

        @pl.when(src < 0)
        def _():
            out[i] = jnp.zeros(out.shape[1:], BF16)

        @pl.when(src >= 0)
        def _():
            out[i] = de[src]

        return carry

    lax.fori_loop(0, out.shape[0], place, 0)


def attend(tab, inv, kb, vb, q, dc, wk, wv):
    width = wk.shape[0]
    same = jax.ShapeDtypeStruct(q.shape, BF16)
    flat = pltpu.HBM(kb.shape, BF16)
    return pl.pallas_call(
        attend_kernel,
        in_specs=[SMEM, SMEM] + [VMEM] * 6,
        out_specs=[VMEM] * 5,
        out_shape=[same, same, flat, flat, pltpu.HBM((inv.shape[0], NLEN, width), BF16)],
        scratch_shapes=[pltpu.VMEM((2 * KMAX, NLEN, width), BF16)],
        cost_estimate=cost(2048 * 896 * 1024, 40 << 20),
        compiler_params=pltpu.CompilerParams(vmem_limit_bytes=34 << 20),
        name="attend",
    )(tab, inv, kb, vb, q, dc, wk, wv)


def finish_kernel(n_ref, x, hid, dout, gain, rstd, stat, wq, wo, out, dhid, oa, na):
    step = pl.program_id(0)
    tokens = hid.shape[0]
    o_part = jnp.concatenate([dot(x[0, :tokens], wo[s, 0], NT) for s in range(4)], axis=1)
    dq = x[0, tokens : 2 * tokens]
    n_part = jnp.concatenate([dot(dq, wq[s, 0], NT) for s in range(4)], axis=1)

    @pl.when(step == 0)
    def _():
        oa[...] = o_part
        na[...] = n_part

    @pl.when((step > 0) & (step < 3))
    def _():
        oa[...] += o_part
        na[...] += n_part

    @pl.when(step == 3)
    def _():
        own = hid[...].astype(F32)
        scale = rstd[...]
        out[...] = (own + (oa[...] + o_part)).astype(BF16)
        scaled = gain[...].astype(F32) * (na[...] + n_part)
        grad = dout[...].astype(F32) + scale * scaled - own * (scale * scale * scale) * stat[...]
        dhid[...] = grad.astype(BF16)


def finish(n, x, hidden, dout, gain, rstd, stat, weights):
    tokens, feats = hidden.shape
    whole = pl.BlockSpec((tokens, feats), lambda r, n: (0, 0))
    column = pl.BlockSpec((tokens, 1), lambda r, n: (0, 0))
    return pl.pallas_call(
        finish_kernel,
        grid_spec=pltpu.PrefetchScalarGridSpec(
            num_scalar_prefetch=1,
            grid=(4,),
            in_specs=[
                pl.BlockSpec((1, x.shape[1], 512), lambda r, n: (r, 0, 0)),
                whole,
                whole,
                pl.BlockSpec((1, feats), lambda r, n: (0, 0)),
                column,
                column,
                pl.BlockSpec((4, 1, 256, 512), lambda r, n: ((2 * n[0] + r) % 4, 0, 0, 0)),
                pl.BlockSpec((4, 1, 256, 512), lambda r, n: ((4 - r) % 4, 1, 0, 0)),
            ],
            out_specs=[whole, whole],
            scratch_shapes=[pltpu.VMEM((tokens, feats), F32)] * 2,
        ),
        out_shape=[jax.ShapeDtypeStruct((tokens, feats), BF16)] * 2,
        cost_estimate=cost(2 * tokens * 4096 * 512, 12 << 20),
        compiler_params=pltpu.CompilerParams(vmem_limit_bytes=24 << 20),
        name="finish",
    )(n, x, hidden, dout, gain[None], rstd, stat, weights, weights)


def outer_kernel(dest, n_ref, d, ctx, o0, o1, o2, o3):
    for i, out in enumerate((o0, o1, o2, o3)):

        def share(j, carry, i=i, out=out):
            to = dest[4 * i + j]
            block = lax.rem(to // 4 + 4 - n_ref[0], 4)
            first = pl.multiple_of(lax.rem(to, 4) * 256, 256)
            out[j] = dot(d[block, :, pl.ds(first, 256)], ctx[...], TN).astype(BF16)
            return carry

        lax.fori_loop(0, 4, share, 0)


def outer(dest, n, dout, ctx):
    share = jax.ShapeDtypeStruct((4, 256, ctx.shape[1]), BF16)
    return pl.pallas_call(
        outer_kernel,
        in_specs=[SMEM, SMEM, VMEM, VMEM],
        out_specs=[VMEM] * 4,
        out_shape=[share] * 4,
        cost_estimate=cost(ctx.shape[0] * 4096 * 512, 6 << 20),
        compiler_params=pltpu.CompilerParams(vmem_limit_bytes=16 << 20),
        name="outer",
    )(dest, n, dout, ctx)


def order_kernel(dest, wk, wv, o0, o1, o2, o3):
    for i, out in enumerate((o0, o1, o2, o3)):
        for j in range(4):
            out[j, 0] = wk[dest[4 * i + j]]
            out[j, 1] = wv[dest[4 * i + j]]


def order(dest, wk, wv):
    share = jax.ShapeDtypeStruct((4, 2) + wk.shape[1:], BF16)
    return pl.pallas_call(
        order_kernel,
        in_specs=[SMEM, VMEM, VMEM],
        out_specs=[VMEM] * 4,
        out_shape=[share] * 4,
        cost_estimate=cost(0, 4 << 20),
        compiler_params=pltpu.CompilerParams(vmem_limit_bytes=16 << 20),
        name="order",
    )(dest, wk, wv)


def along(share, by, first):
    pairs = []
    for i in range(16):
        for core in range(2):
            x, z = i // 4, i % 4
            if (core == 0) == first:
                x = (x + by) % 4
            else:
                z = (z + by) % 4
            pairs.append((2 * i + core, 2 * (4 * x + z) + core))
    return lax.ppermute(share, ("seq", "batch"), pairs)


def first_phase(shares):
    return [shares[0]] + [along(shares[i], i, True) for i in (2, 1, 3)]


def second_phase(arrived):
    near = total(arrived).astype(BF16)
    return total([near[0]] + [along(near[j], j, False) for j in (2, 1, 3)])


def slot_tables(slot_span, n):
    slots = slot_span.shape[0]
    ids = jnp.arange(slots, dtype=jnp.int32)
    before = ids[None, :] < ids[:, None]
    same = slot_span[None, :] == slot_span[:, None]
    rank = jnp.sum(same & before, axis=1, dtype=jnp.int32)
    where = jnp.where(slot_span >= 0, slot_span * KMAX + rank, -1).astype(jnp.int32)
    spot = jnp.arange(2 * KMAX, dtype=jnp.int32)
    hit = where[None, :] == spot[:, None]
    relative = (ids + slots - 6 * n) % slots
    source = jnp.sum(jnp.where(hit, relative[None, :] + 1, 0), axis=1, dtype=jnp.int32) - 1
    counts = jnp.sum(slot_span[None, :] == jnp.arange(2)[:, None], axis=1, dtype=jnp.int32)
    return jnp.concatenate([source, counts]), where


def body(hidden, d_out, nbr_emb, slot_span, dec_gain, enc_gain, w_cond, w_enc, w_q, w_k, w_v, w_o):
    n = lax.axis_index("nbr")
    b = lax.axis_index("batch")
    n1 = n.astype(jnp.int32).reshape(1)
    tokens, feats = hidden.shape
    spans = tokens // CLEN

    kv_half = jnp.where(b == 0, w_k, w_v)
    swap = []
    for i in range(4):
        for j in range(4):
            for k in range(4):
                for core, x in ((0, (i + k) % 4), (1, (i - k) % 4)):
                    swap.append((((4 * i + j) * 4 + k) * 2 + core, ((4 * x + j) * 4 + i) * 2 + core))
    qo_half = lax.ppermute(
        jnp.where(b == 0, w_q, w_o.T), ("seq", "nbr", "batch"), swap
    )
    weights = lax.all_gather(
        jnp.concatenate([qo_half, kv_half], axis=0), ("seq", "batch"), axis=0
    )

    hf = hidden.astype(F32)
    pooled = jnp.mean(hf.reshape(spans, CLEN, feats), axis=1).astype(BF16)
    squares = jnp.sum(hf * hf, axis=-1)
    length = lax.axis_size("seq")
    carried = lax.ppermute(
        pooled[spans - 1 :], "seq", [(i, i + 1) for i in range(length - 1)]
    )
    previous = jnp.concatenate([carried, pooled[: spans - 1]], axis=0)
    width = nbr_emb.shape[2]
    small = jnp.concatenate(
        [
            jnp.dot(previous, w_cond, preferred_element_type=F32),
            jnp.pad(squares, (0, width - tokens))[None],
        ],
        axis=0,
    )
    small = sum_small(small)
    condition = small[:spans]
    rstd = lax.rsqrt(small[spans, :tokens] / (4 * feats) + 1e-06)[:, None]
    normed = (hf * rstd * dec_gain.astype(F32)).astype(BF16)

    nbr_emb = lax.optimization_barrier((nbr_emb, condition))[0]
    e1, e2a, e2b, e3 = ring_gather(nbr_emb)
    later = lax.optimization_barrier((d_out, e1, e3))[0]
    d2, d1, d3 = (shift(later, r) for r in (2, -1, 1))
    dout_rel = jnp.stack([d_out, d1, d2, d3])

    tab, inv = slot_tables(slot_span, n)
    rel_span = jnp.roll(slot_span.reshape(4, 6), -n, axis=0).reshape(-1)

    def encode(block, first):
        own = lax.slice_in_dim(rel_span, first, first + block.shape[0])
        own = own[:, None, None]
        cond = jnp.where(own == 0, condition[0], jnp.where(own == 1, condition[1], 0.0))
        x = block.astype(F32) + cond
        enc_normed = (x * rms_scale(x) * enc_gain.astype(F32)).astype(BF16)
        width = x.shape[2]
        mixed = jnp.dot(
            enc_normed.reshape(-1, width), w_enc, preferred_element_type=F32
        ).reshape(x.shape)
        return (x + jax.nn.silu(mixed)).astype(BF16)


    pairs = weights.reshape(16, 2, 312, 512)
    weights = pltpu.with_memory_space_constraint(pairs, pltpu.HBM)
    wk = pairs[:, 0, 256:].reshape(-1, 512)
    wv = pairs[:, 1, 256:].reshape(-1, 512)

    normed, dout_rel = lax.optimization_barrier((normed, dout_rel))
    shares = scattered(project(n1, normed, d_out, weights))
    both = total(shares).astype(BF16)
    query, d_ctx = both[:tokens], both[tokens:]
    e2 = jnp.concatenate([e2a, e2b], axis=0)
    encoded = [encode(nbr_emb, 0), encode(e1, 6), encode(e2, 12), encode(e3, 18)]
    enc, keys, values = keys_values(tab, encoded, wk, wv)
    ctx, d_query, d_key, d_value, parts = attend(
        tab, inv, keys, values, query, d_ctx, wk, wv
    )
    d_enc = lax.psum_scatter(parts, "nbr", scatter_dimension=0, tiled=True)

    inner = jnp.sum(d_query.astype(F32) * query.astype(F32), axis=-1).astype(BF16)
    more = jnp.broadcast_to(jnp.pad(inner, (0, ctx.shape[1] - tokens))[None], (16, ctx.shape[1]))
    local = jnp.concatenate([ctx, d_query, more], axis=0)
    heads = jnp.stack([local, shift(local, -1), shift(local, 2), shift(local, 1)])
    stat = jnp.sum(heads[:, 2 * tokens, :tokens].astype(F32), axis=0)[:, None]
    stat = stat / (rstd * (4 * feats))
    out, d_hidden = finish(n1, heads, hidden, d_out, dec_gain, rstd, stat, weights)

    place = lax.axis_index("seq")
    step = jnp.arange(4, dtype=jnp.int32)
    one, two = step[:, None], step[None, :]
    by_x, by_z = jnp.where(b == 0, one, two), jnp.where(b == 0, two, one)
    dest = (place // 4 + by_x) % 4 * 4 + (place % 4 + by_z) % 4
    dest = dest.astype(jnp.int32).reshape(-1)
    arrived = first_phase(outer(dest, n1, dout_rel, ctx))
    d_wo = second_phase(arrived).T

    enc = lax.optimization_barrier((enc, arrived[2]))[0]
    rows = enc.reshape(-1, enc.shape[2])
    wk_parts = dot(rows, d_key, TN).astype(BF16).reshape(16, -1, 512)
    wv_parts = dot(rows, d_value, TN).astype(BF16).reshape(16, -1, 512)
    both = second_phase(first_phase(order(dest, wk_parts, wv_parts)))
    d_wk, d_wv = both[0], both[1]

    return (out, d_hidden, d_enc, d_wo, d_wk, d_wv)


def solution(mesh):
    placed = (
        P(("batch", "seq"), "nbr"),
        P(("batch", "seq"), "nbr"),
        P(("batch", "seq", "nbr"), None, None),
        P(("batch", "seq")),
        P("nbr"),
        P(),
        P("nbr", None),
        P(),
        P("seq", "nbr"),
        P("seq", "nbr"),
        P("seq", "nbr"),
        P("nbr", "seq"),
    )
    return jax.shard_map(
        body,
        mesh=mesh,
        in_specs=placed,
        out_specs=(
            P(("batch", "seq"), "nbr"),
            P(("batch", "seq"), "nbr"),
            P(("batch", "seq", "nbr"), None, None),
            P(("batch", "nbr"), "seq"),
            P(("batch", "seq"), "nbr"),
            P(("batch", "seq"), "nbr"),
        ),
        check_vma=False,
    )
```

```python
import jax
import jax.numpy as jnp
from jax import lax
from jax.experimental import pallas as pl
from jax.experimental.pallas import tpu as pltpu
from jax.sharding import PartitionSpec as P

HD = 128
CLEN = 64
NLEN = 128
KMAX = 8
F32 = jnp.float32
BF16 = jnp.bfloat16
VMEM = pl.BlockSpec(memory_space=pltpu.VMEM)
SMEM = pl.BlockSpec(memory_space=pltpu.SMEM)


def dot(a, b, dims=((1,), (0,))):
    return lax.dot_general(a, b, (dims, ((), ())), preferred_element_type=F32)


NT = ((1,), (1,))
TN = ((0,), (0,))


def shift(x, by):
    n = lax.axis_size("nbr")
    return lax.ppermute(x, "nbr", [(i, (i + by) % n) for i in range(n)])


def ring_gather(x):
    half = x.shape[0] // 2
    right = shift(x, -1)
    left = shift(x, 1)
    far_a = shift(right[:half], -1)
    far_b = shift(left[half:], 1)
    return right, far_a, far_b, left


def scattered(parts):
    return [parts[0]] + [shift(parts[r], r) for r in (2, 1, 3)]


def total(shares):
    return sum(x.astype(F32) for x in shares)


def sum_small(x):
    return x + shift(x, 1) + shift(x, 2) + shift(x, 3)


def rms_scale(values):
    return lax.rsqrt(jnp.mean(values * values, axis=-1, keepdims=True) + 1e-06)


def cost(products, moved):
    return pl.CostEstimate(flops=2 * products, transcendentals=0, bytes_accessed=moved)


def project_kernel(n_ref, x, d, wq, wo, o):
    tokens = x.shape[0]
    q = jnp.zeros((tokens, 512), F32)
    dc = jnp.zeros((tokens, 512), F32)
    for s in range(4):
        cols = slice(256 * s, 256 * s + 256)
        q += dot(x[:, cols], wq[s, 0])
        dc += dot(d[:, cols], wo[s, 0])
    o[0, :tokens] = q.astype(BF16)
    o[0, tokens:] = dc.astype(BF16)


def project(n, normed, dout, weights):
    tokens, feats = normed.shape
    return pl.pallas_call(
        project_kernel,
        grid_spec=pltpu.PrefetchScalarGridSpec(
            num_scalar_prefetch=1,
            grid=(4,),
            in_specs=[
                pl.BlockSpec((tokens, feats), lambda r, n: (0, 0)),
                pl.BlockSpec((tokens, feats), lambda r, n: (0, 0)),
                pl.BlockSpec((4, 1, 256, 512), lambda r, n: ((2 * n[0] + r) % 4, 0, 0, 0)),
                pl.BlockSpec((4, 1, 256, 512), lambda r, n: ((4 - r) % 4, 1, 0, 0)),
            ],
            out_specs=pl.BlockSpec((1, 2 * tokens, 512), lambda r, n: (r, 0, 0)),
        ),
        out_shape=jax.ShapeDtypeStruct((4, 2 * tokens, 512), BF16),
        cost_estimate=cost(2 * tokens * 4096 * 512, 12 << 20),
        compiler_params=pltpu.CompilerParams(vmem_limit_bytes=24 << 20),
        name="project",
    )(n, normed, dout, weights, weights)


def keys_kernel(tab, e0, near, far, wk, wv, enc, kb, vb):
    tables = ((e0, 0, 6, 0), (near, 6, 12, 0), (far, 12, 18, 0), (near, 18, 24, 6))

    def pick(j, carry):
        src = tab[j]

        @pl.when(src < 0)
        def _():
            enc[j] = jnp.zeros(enc.shape[1:], BF16)

        for ref, first, end, base in tables:

            @pl.when((src >= first) & (src < end))
            def _(ref=ref, first=first, base=base):
                enc[j] = ref[src - first + base]

        return carry

    lax.fori_loop(0, 2 * KMAX, pick, 0)

    def kv(c, carry):
        x = enc[pl.ds(4 * c, 4)].reshape(4 * NLEN, enc.shape[2])
        rows = pl.ds(pl.multiple_of(c * 512, 512), 512)
        kb[rows, :] = dot(x, wk[...]).astype(BF16)
        vb[rows, :] = dot(x, wv[...]).astype(BF16)
        return carry

    lax.fori_loop(0, 4, kv, 0)


def keys_values(tab, blocks, wk, wv):
    rows = 2 * KMAX * NLEN
    flat = jax.ShapeDtypeStruct((rows, wk.shape[1]), BF16)
    return pl.pallas_call(
        keys_kernel,
        in_specs=[SMEM] + [VMEM] * 5,
        out_specs=[VMEM] * 3,
        out_shape=[pltpu.HBM((2 * KMAX, NLEN, wk.shape[0]), BF16), flat, flat],
        cost_estimate=cost(2048 * 896 * 1024, 16 << 20),
        compiler_params=pltpu.CompilerParams(vmem_limit_bytes=26 << 20),
        name="keys_values",
    )(tab, *blocks, wk, wv)


def attend_kernel(tab, inv, kb, vb, q, dc, wk, wv, ctx, dq, dk, dv, out, de):
    factor = HD ** (-0.5)
    heads = q.shape[1] // HD
    keys = KMAX * NLEN
    for c in range(2):
        limit = tab[2 * KMAX + c] * NLEN
        allowed = lax.broadcasted_iota(jnp.int32, (CLEN, keys), 1) < limit
        toks = slice(c * CLEN, (c + 1) * CLEN)
        rows = slice(c * keys, (c + 1) * keys)
        for h in range(heads):
            cols = slice(h * HD, (h + 1) * HD)
            qh, dh = q[toks, cols], dc[toks, cols]
            s = jnp.where(allowed, dot(qh, kb[rows, cols], NT) * factor, -1e30)
            w = jnp.exp(s - jnp.max(s, axis=-1, keepdims=True))
            p = w / jnp.sum(w, axis=-1, keepdims=True)
            pb = p.astype(BF16)
            ctx[toks, cols] = dot(pb, vb[rows, cols]).astype(BF16)
            dp = dot(dh, vb[rows, cols], NT)
            rd = jnp.sum(p * dp, axis=-1, keepdims=True)
            ds = (p * (dp - rd) * factor).astype(BF16)
            dq[toks, cols] = dot(ds, kb[rows, cols]).astype(BF16)
            dk[rows, cols] = dot(ds, qh, TN).astype(BF16)
            dv[rows, cols] = dot(pb, dh, TN).astype(BF16)

    def grad(c, carry):
        rows = pl.ds(pl.multiple_of(c * 512, 512), 512)
        part = dot(dk[rows, :], wk[...], NT) + dot(dv[rows, :], wv[...], NT)
        de[pl.ds(4 * c, 4)] = part.astype(BF16).reshape(4, NLEN, wk.shape[0])
        return carry

    lax.fori_loop(0, 4, grad, 0)

    def place(i, carry):
        src = inv[i]

        @pl.when(src < 0)
        def _():
            out[i] = jnp.zeros(out.shape[1:], BF16)

        @pl.when(src >= 0)
        def _():
            out[i] = de[src]

        return carry

    lax.fori_loop(0, out.shape[0], place, 0)


def attend(tab, inv, kb, vb, q, dc, wk, wv):
    width = wk.shape[0]
    same = jax.ShapeDtypeStruct(q.shape, BF16)
    flat = pltpu.HBM(kb.shape, BF16)
    return pl.pallas_call(
        attend_kernel,
        in_specs=[SMEM, SMEM] + [VMEM] * 6,
        out_specs=[VMEM] * 5,
        out_shape=[same, same, flat, flat, pltpu.HBM((inv.shape[0], NLEN, width), BF16)],
        scratch_shapes=[pltpu.VMEM((2 * KMAX, NLEN, width), BF16)],
        cost_estimate=cost(2048 * 896 * 1024, 40 << 20),
        compiler_params=pltpu.CompilerParams(vmem_limit_bytes=34 << 20),
        name="attend",
    )(tab, inv, kb, vb, q, dc, wk, wv)


def finish_kernel(n_ref, x, hid, dout, gain, rstd, stat, wq, wo, out, dhid, oa, na):
    step = pl.program_id(0)
    tokens = hid.shape[0]
    o_part = jnp.concatenate([dot(x[0, :tokens], wo[s, 0], NT) for s in range(4)], axis=1)
    dq = x[0, tokens : 2 * tokens]
    n_part = jnp.concatenate([dot(dq, wq[s, 0], NT) for s in range(4)], axis=1)

    @pl.when(step == 0)
    def _():
        oa[...] = o_part
        na[...] = n_part

    @pl.when((step > 0) & (step < 3))
    def _():
        oa[...] += o_part
        na[...] += n_part

    @pl.when(step == 3)
    def _():
        own = hid[...].astype(F32)
        scale = rstd[...]
        out[...] = (own + (oa[...] + o_part)).astype(BF16)
        scaled = gain[...].astype(F32) * (na[...] + n_part)
        grad = dout[...].astype(F32) + scale * scaled - own * (scale * scale * scale) * stat[...]
        dhid[...] = grad.astype(BF16)


def finish(n, x, hidden, dout, gain, rstd, stat, weights):
    tokens, feats = hidden.shape
    whole = pl.BlockSpec((tokens, feats), lambda r, n: (0, 0))
    column = pl.BlockSpec((tokens, 1), lambda r, n: (0, 0))
    return pl.pallas_call(
        finish_kernel,
        grid_spec=pltpu.PrefetchScalarGridSpec(
            num_scalar_prefetch=1,
            grid=(4,),
            in_specs=[
                pl.BlockSpec((1, x.shape[1], 512), lambda r, n: (r, 0, 0)),
                whole,
                whole,
                pl.BlockSpec((1, feats), lambda r, n: (0, 0)),
                column,
                column,
                pl.BlockSpec((4, 1, 256, 512), lambda r, n: ((2 * n[0] + r) % 4, 0, 0, 0)),
                pl.BlockSpec((4, 1, 256, 512), lambda r, n: ((4 - r) % 4, 1, 0, 0)),
            ],
            out_specs=[whole, whole],
            scratch_shapes=[pltpu.VMEM((tokens, feats), F32)] * 2,
        ),
        out_shape=[jax.ShapeDtypeStruct((tokens, feats), BF16)] * 2,
        cost_estimate=cost(2 * tokens * 4096 * 512, 12 << 20),
        compiler_params=pltpu.CompilerParams(vmem_limit_bytes=24 << 20),
        name="finish",
    )(n, x, hidden, dout, gain[None], rstd, stat, weights, weights)


def pack_kernel(dest, n_ref, d, ctx, wk, wv, o0, o1, o2, o3):
    rows = wk.shape[1]
    for i, out in enumerate((o0, o1, o2, o3)):

        def share(j, carry, i=i, out=out):
            to = dest[4 * i + j]
            block = lax.rem(to // 4 + 4 - n_ref[0], 4)
            first = pl.multiple_of(lax.rem(to, 4) * 256, 256)
            part = dot(d[block, :, pl.ds(first, 256)], ctx[...], TN)
            out[j, 0:256] = part.astype(BF16)
            out[j, 256 : 256 + rows] = wk[to]
            out[j, 320 : 320 + rows] = wv[to]
            return carry

        lax.fori_loop(0, 4, share, 0)


def pack(dest, n, dout, ctx, wk, wv):
    share = jax.ShapeDtypeStruct((4, 384, ctx.shape[1]), BF16)
    return pl.pallas_call(
        pack_kernel,
        in_specs=[SMEM, SMEM, VMEM, VMEM, VMEM, VMEM],
        out_specs=[VMEM] * 4,
        out_shape=[share] * 4,
        cost_estimate=cost(ctx.shape[0] * 4096 * 512, 16 << 20),
        compiler_params=pltpu.CompilerParams(vmem_limit_bytes=24 << 20),
        name="pack",
    )(dest, n, dout, ctx, wk, wv)


def along(share, by, first):
    pairs = []
    for i in range(16):
        for core in range(2):
            x, z = i // 4, i % 4
            if (core == 0) == first:
                x = (x + by) % 4
            else:
                z = (z + by) % 4
            pairs.append((2 * i + core, 2 * (4 * x + z) + core))
    return lax.ppermute(share, ("seq", "batch"), pairs)


def first_phase(shares):
    return [shares[0]] + [along(shares[i], i, True) for i in (2, 1, 3)]


def second_phase(near):
    return total([near[0]] + [along(near[j], j, False) for j in (2, 1, 3)])


def slot_tables(slot_span, n):
    slots = slot_span.shape[0]
    ids = jnp.arange(slots, dtype=jnp.int32)
    before = ids[None, :] < ids[:, None]
    same = slot_span[None, :] == slot_span[:, None]
    rank = jnp.sum(same & before, axis=1, dtype=jnp.int32)
    where = jnp.where(slot_span >= 0, slot_span * KMAX + rank, -1).astype(jnp.int32)
    spot = jnp.arange(2 * KMAX, dtype=jnp.int32)
    hit = where[None, :] == spot[:, None]
    relative = (ids + slots - 6 * n) % slots
    source = jnp.sum(jnp.where(hit, relative[None, :] + 1, 0), axis=1, dtype=jnp.int32) - 1
    counts = jnp.sum(slot_span[None, :] == jnp.arange(2)[:, None], axis=1, dtype=jnp.int32)
    return jnp.concatenate([source, counts]), where


def body(hidden, d_out, nbr_emb, slot_span, dec_gain, enc_gain, w_cond, w_enc, w_q, w_k, w_v, w_o):
    n = lax.axis_index("nbr")
    b = lax.axis_index("batch")
    n1 = n.astype(jnp.int32).reshape(1)
    tokens, feats = hidden.shape
    spans = tokens // CLEN

    kv_half = jnp.where(b == 0, w_k, w_v)
    swap = []
    for i in range(4):
        for j in range(4):
            for k in range(4):
                for core, x in ((0, (i + k) % 4), (1, (i - k) % 4)):
                    swap.append((((4 * i + j) * 4 + k) * 2 + core, ((4 * x + j) * 4 + i) * 2 + core))
    qo_half = lax.ppermute(
        jnp.where(b == 0, w_q, w_o.T), ("seq", "nbr", "batch"), swap
    )
    weights = lax.all_gather(
        jnp.concatenate([qo_half, kv_half], axis=0), ("seq", "batch"), axis=0
    )

    hf = hidden.astype(F32)
    pooled = jnp.mean(hf.reshape(spans, CLEN, feats), axis=1).astype(BF16)
    squares = jnp.sum(hf * hf, axis=-1)
    length = lax.axis_size("seq")
    carried = lax.ppermute(
        pooled[spans - 1 :], "seq", [(i, i + 1) for i in range(length - 1)]
    )
    previous = jnp.concatenate([carried, pooled[: spans - 1]], axis=0)
    width = nbr_emb.shape[2]
    small = jnp.concatenate(
        [
            jnp.dot(previous, w_cond, preferred_element_type=F32),
            jnp.pad(squares, (0, width - tokens))[None],
        ],
        axis=0,
    )
    small = sum_small(small)
    condition = small[:spans]
    rstd = lax.rsqrt(small[spans, :tokens] / (4 * feats) + 1e-06)[:, None]
    normed = (hf * rstd * dec_gain.astype(F32)).astype(BF16)

    nbr_emb = lax.optimization_barrier((nbr_emb, condition))[0]
    e1, e2a, e2b, e3 = ring_gather(nbr_emb)

    tab, inv = slot_tables(slot_span, n)
    rel_span = jnp.roll(slot_span.reshape(4, 6), -n, axis=0).reshape(-1)

    def encode(block, own):
        own = own[:, None, None]
        cond = jnp.where(own == 0, condition[0], jnp.where(own == 1, condition[1], 0.0))
        x = block.astype(F32) + cond
        enc_normed = (x * rms_scale(x) * enc_gain.astype(F32)).astype(BF16)
        width = x.shape[2]
        mixed = jnp.dot(
            enc_normed.reshape(-1, width), w_enc, preferred_element_type=F32
        ).reshape(x.shape)
        return (x + jax.nn.silu(mixed)).astype(BF16)


    pairs = weights.reshape(16, 2, 312, 512)
    weights = pltpu.with_memory_space_constraint(pairs, pltpu.HBM)
    wk = pairs[:, 0, 256:].reshape(-1, 512)
    wv = pairs[:, 1, 256:].reshape(-1, 512)

    shares = project(n1, normed, d_out, weights)
    both = total(scattered(shares)).astype(BF16)
    later = lax.optimization_barrier((d_out, both))[0]
    d2, d1, d3 = (shift(later, r) for r in (2, -1, 1))
    query, d_ctx = both[:tokens], both[tokens:]
    near = jnp.concatenate([e1, e3], axis=0)
    far = jnp.concatenate([e2a, e2b], axis=0)
    encoded = [
        encode(nbr_emb, rel_span[:6]),
        encode(near, jnp.concatenate([rel_span[6:12], rel_span[18:]])),
        encode(far, rel_span[12:18]),
    ]
    enc, keys, values = keys_values(tab, encoded, wk, wv)
    ctx, d_query, d_key, d_value, parts = attend(
        tab, inv, keys, values, query, d_ctx, wk, wv
    )
    parts, d1, d2, d3 = lax.optimization_barrier((parts, d1, d2, d3))
    dout_rel = jnp.stack([d_out, d1, d2, d3])
    d_enc = lax.psum_scatter(parts, "nbr", scatter_dimension=0, tiled=True)

    place = lax.axis_index("seq")
    step = jnp.arange(4, dtype=jnp.int32)
    one, two = step[:, None], step[None, :]
    by_x, by_z = jnp.where(b == 0, one, two), jnp.where(b == 0, two, one)
    dest = (place // 4 + by_x) % 4 * 4 + (place % 4 + by_z) % 4
    dest = dest.astype(jnp.int32).reshape(-1)
    rows = enc.reshape(-1, enc.shape[2])
    wk_parts = dot(rows, d_key, TN).astype(BF16).reshape(16, -1, 512)
    wv_parts = dot(rows, d_value, TN).astype(BF16).reshape(16, -1, 512)
    arrived = first_phase(pack(dest, n1, dout_rel, ctx, wk_parts, wv_parts))
    near = total(arrived).astype(BF16)
    whole = second_phase(near)
    d_wo = whole[:256].T
    d_wk, d_wv = whole[256:312], whole[320:376]

    inner = jnp.sum(d_query.astype(F32) * query.astype(F32), axis=-1).astype(BF16)
    more = jnp.broadcast_to(jnp.pad(inner, (0, ctx.shape[1] - tokens))[None], (16, ctx.shape[1]))
    local = jnp.concatenate([ctx, d_query, more], axis=0)
    heads = jnp.stack([local, shift(local, -1), shift(local, 2), shift(local, 1)])
    heads = lax.optimization_barrier((heads, near))[0]
    stat = jnp.sum(heads[:, 2 * tokens, :tokens].astype(F32), axis=0)[:, None]
    stat = stat / (rstd * (4 * feats))
    out, d_hidden = finish(n1, heads, hidden, d_out, dec_gain, rstd, stat, weights)

    return (out, d_hidden, d_enc, d_wo, d_wk, d_wv)


def solution(mesh):
    placed = (
        P(("batch", "seq"), "nbr"),
        P(("batch", "seq"), "nbr"),
        P(("batch", "seq", "nbr"), None, None),
        P(("batch", "seq")),
        P("nbr"),
        P(),
        P("nbr", None),
        P(),
        P("seq", "nbr"),
        P("seq", "nbr"),
        P("seq", "nbr"),
        P("nbr", "seq"),
    )
    return jax.shard_map(
        body,
        mesh=mesh,
        in_specs=placed,
        out_specs=(
            P(("batch", "seq"), "nbr"),
            P(("batch", "seq"), "nbr"),
            P(("batch", "seq", "nbr"), None, None),
            P(("batch", "nbr"), "seq"),
            P(("batch", "seq"), "nbr"),
            P(("batch", "seq"), "nbr"),
        ),
        check_vma=False,
    )
```

```python
import jax
import jax.numpy as jnp
from jax import lax
from jax.experimental import pallas as pl
from jax.experimental.pallas import tpu as pltpu
from jax.sharding import PartitionSpec as P

HD = 128
CLEN = 64
NLEN = 128
KMAX = 8
F32 = jnp.float32
BF16 = jnp.bfloat16
VMEM = pl.BlockSpec(memory_space=pltpu.VMEM)
SMEM = pl.BlockSpec(memory_space=pltpu.SMEM)


def dot(a, b, dims=((1,), (0,))):
    return lax.dot_general(a, b, (dims, ((), ())), preferred_element_type=F32)


NT = ((1,), (1,))
TN = ((0,), (0,))


def shift(x, by):
    n = lax.axis_size("nbr")
    return lax.ppermute(x, "nbr", [(i, (i + by) % n) for i in range(n)])


def ring_gather(x):
    half = x.shape[0] // 2
    right = shift(x, -1)
    left = shift(x, 1)
    far_a = shift(right[:half], -1)
    far_b = shift(left[half:], 1)
    return right, far_a, far_b, left


def scattered(parts):
    return [parts[0]] + [shift(parts[r], r) for r in (2, 1, 3)]


def total(shares):
    return sum(x.astype(F32) for x in shares)


def sum_small(x):
    return x + shift(x, 1) + shift(x, 2) + shift(x, 3)


def rms_scale(values):
    return lax.rsqrt(jnp.mean(values * values, axis=-1, keepdims=True) + 1e-06)


def cost(products, moved):
    return pl.CostEstimate(flops=2 * products, transcendentals=0, bytes_accessed=moved)


def project_kernel(n_ref, x, d, wq, wo, o):
    tokens = x.shape[0]
    q = jnp.zeros((tokens, 512), F32)
    dc = jnp.zeros((tokens, 512), F32)
    for s in range(4):
        cols = slice(256 * s, 256 * s + 256)
        q += dot(x[:, cols], wq[s, 0])
        dc += dot(d[:, cols], wo[s, 0])
    o[0, :tokens] = q.astype(BF16)
    o[0, tokens:] = dc.astype(BF16)


def project(n, normed, dout, weights):
    tokens, feats = normed.shape
    return pl.pallas_call(
        project_kernel,
        grid_spec=pltpu.PrefetchScalarGridSpec(
            num_scalar_prefetch=1,
            grid=(4,),
            in_specs=[
                pl.BlockSpec((tokens, feats), lambda r, n: (0, 0)),
                pl.BlockSpec((tokens, feats), lambda r, n: (0, 0)),
                pl.BlockSpec((4, 1, 256, 512), lambda r, n: ((n[0] + 6 - r) % 4, 0, 0, 0)),
                pl.BlockSpec((4, 1, 256, 512), lambda r, n: ((n[0] + 6 - r) % 4, 1, 0, 0)),
            ],
            out_specs=pl.BlockSpec((1, 2 * tokens, 512), lambda r, n: (r, 0, 0)),
        ),
        out_shape=jax.ShapeDtypeStruct((4, 2 * tokens, 512), BF16),
        cost_estimate=cost(2 * tokens * 4096 * 512, 12 << 20),
        compiler_params=pltpu.CompilerParams(vmem_limit_bytes=12 << 20),
        name="project",
    )(n, normed, dout, weights, weights)


def keys_kernel(tab, e0, near, far, wk, wv, enc, kb, vb):
    tables = ((e0, 0, 6, 0), (near, 6, 12, 0), (far, 12, 18, 0), (near, 18, 24, 6))

    def pick(j, carry):
        src = tab[j]

        @pl.when(src < 0)
        def _():
            enc[j] = jnp.zeros(enc.shape[1:], BF16)

        for ref, first, end, base in tables:

            @pl.when((src >= first) & (src < end))
            def _(ref=ref, first=first, base=base):
                enc[j] = ref[src - first + base]

        return carry

    lax.fori_loop(0, 2 * KMAX, pick, 0)

    def kv(c, carry):
        x = enc[pl.ds(4 * c, 4)].reshape(4 * NLEN, enc.shape[2])
        rows = pl.ds(pl.multiple_of(c * 512, 512), 512)
        kb[rows, :] = dot(x, wk[...]).astype(BF16)
        vb[rows, :] = dot(x, wv[...]).astype(BF16)
        return carry

    lax.fori_loop(0, 4, kv, 0)


def keys_values(tab, blocks, wk, wv):
    rows = 2 * KMAX * NLEN
    flat = jax.ShapeDtypeStruct((rows, wk.shape[1]), BF16)
    return pl.pallas_call(
        keys_kernel,
        in_specs=[SMEM] + [VMEM] * 5,
        out_specs=[VMEM] * 3,
        out_shape=[pltpu.HBM((2 * KMAX, NLEN, wk.shape[0]), BF16), flat, flat],
        cost_estimate=cost(2048 * 896 * 1024, 16 << 20),
        compiler_params=pltpu.CompilerParams(vmem_limit_bytes=22 << 20),
        name="keys_values",
    )(tab, *blocks, wk, wv)


def attend_kernel(tab, inv, kb, vb, q, dc, wk, wv, ctx, dq, dk_out, dv_out, out, dk, dv, de, blank, sems):
    slots = out.shape[0]
    blank[...] = jnp.zeros(blank.shape, BF16)

    def to_slot(i, source):
        return pltpu.make_async_copy(source, out.at[i], sems.at[i])

    def empty(i, carry):
        @pl.when(inv[i] < 0)
        def _():
            to_slot(i, blank).start()

        return carry

    lax.fori_loop(0, slots, empty, 0)
    factor = HD ** (-0.5)
    heads = q.shape[1] // HD
    keys = KMAX * NLEN
    for c in range(2):
        limit = tab[2 * KMAX + c] * NLEN
        allowed = lax.broadcasted_iota(jnp.int32, (CLEN, keys), 1) < limit
        toks = slice(c * CLEN, (c + 1) * CLEN)
        rows = slice(c * keys, (c + 1) * keys)
        for h in range(heads):
            cols = slice(h * HD, (h + 1) * HD)
            qh, dh = q[toks, cols], dc[toks, cols]
            s = jnp.where(allowed, dot(qh, kb[rows, cols], NT) * factor, -1e30)
            w = jnp.exp(s - jnp.max(s, axis=-1, keepdims=True))
            p = w / jnp.sum(w, axis=-1, keepdims=True)
            pb = p.astype(BF16)
            ctx[toks, cols] = dot(pb, vb[rows, cols]).astype(BF16)
            dp = dot(dh, vb[rows, cols], NT)
            rd = jnp.sum(p * dp, axis=-1, keepdims=True)
            ds = (p * (dp - rd) * factor).astype(BF16)
            dq[toks, cols] = dot(ds, kb[rows, cols]).astype(BF16)
            dk[rows, cols] = dot(ds, qh, TN).astype(BF16)
            dv[rows, cols] = dot(pb, dh, TN).astype(BF16)

    copies = [
        pltpu.make_async_copy(dk, dk_out, sems.at[slots]),
        pltpu.make_async_copy(dv, dv_out, sems.at[slots + 1]),
    ]
    for copy in copies:
        copy.start()

    def grad(c, carry):
        rows = pl.ds(pl.multiple_of(c * 512, 512), 512)
        part = dot(dk[rows, :], wk[...], NT) + dot(dv[rows, :], wv[...], NT)
        de[pl.ds(4 * c, 4)] = part.astype(BF16).reshape(4, NLEN, wk.shape[0])

        def send(i, carry):
            src = inv[i]

            @pl.when((src >= 4 * c) & (src < 4 * c + 4))
            def _():
                to_slot(i, de.at[src]).start()

            return carry

        return lax.fori_loop(0, slots, send, carry)

    lax.fori_loop(0, 4, grad, 0)

    def arrive(i, carry):
        to_slot(i, blank).wait()
        return carry

    lax.fori_loop(0, slots, arrive, 0)
    for copy in copies:
        copy.wait()


def attend(tab, inv, kb, vb, q, dc, wk, wv):
    width = wk.shape[0]
    same = jax.ShapeDtypeStruct(q.shape, BF16)
    flat = pltpu.HBM(kb.shape, BF16)
    return pl.pallas_call(
        attend_kernel,
        in_specs=[SMEM, SMEM] + [VMEM] * 6,
        out_specs=[VMEM] * 2 + [pl.BlockSpec(memory_space=pl.ANY)] * 3,
        out_shape=[same, same, flat, flat, pltpu.HBM((inv.shape[0], NLEN, width), BF16)],
        scratch_shapes=[
            pltpu.VMEM(kb.shape, BF16),
            pltpu.VMEM(kb.shape, BF16),
            pltpu.VMEM((2 * KMAX, NLEN, width), BF16),
            pltpu.VMEM((NLEN, width), BF16),
            pltpu.SemaphoreType.DMA((inv.shape[0] + 2,)),
        ],
        cost_estimate=cost(2048 * 896 * 1024, 40 << 20),
        compiler_params=pltpu.CompilerParams(vmem_limit_bytes=24 << 20),
        name="attend",
    )(tab, inv, kb, vb, q, dc, wk, wv)


def finish_kernel(n_ref, x, hid, dout, gain, rstd, stat, wq, wo, out, dhid, oa, na):
    step = pl.program_id(0)
    tokens = hid.shape[0]
    o_part = jnp.concatenate([dot(x[0, :tokens], wo[s, 0], NT) for s in range(4)], axis=1)
    dq = x[0, tokens : 2 * tokens]
    n_part = jnp.concatenate([dot(dq, wq[s, 0], NT) for s in range(4)], axis=1)

    @pl.when(step == 0)
    def _():
        oa[...] = o_part
        na[...] = n_part

    @pl.when((step > 0) & (step < 3))
    def _():
        oa[...] += o_part
        na[...] += n_part

    @pl.when(step == 3)
    def _():
        own = hid[...].astype(F32)
        scale = rstd[...]
        out[...] = (own + (oa[...] + o_part)).astype(BF16)
        scaled = gain[...].astype(F32) * (na[...] + n_part)
        grad = dout[...].astype(F32) + scale * scaled - own * (scale * scale * scale) * stat[...]
        dhid[...] = grad.astype(BF16)


def finish(n, x, hidden, dout, gain, rstd, stat, weights):
    tokens, feats = hidden.shape
    whole = pl.BlockSpec((tokens, feats), lambda r, n: (0, 0))
    column = pl.BlockSpec((tokens, 1), lambda r, n: (0, 0))
    return pl.pallas_call(
        finish_kernel,
        grid_spec=pltpu.PrefetchScalarGridSpec(
            num_scalar_prefetch=1,
            grid=(4,),
            in_specs=[
                pl.BlockSpec((1, x.shape[1], 512), lambda r, n: (r, 0, 0)),
                whole,
                whole,
                pl.BlockSpec((1, feats), lambda r, n: (0, 0)),
                column,
                column,
                pl.BlockSpec((4, 1, 256, 512), lambda r, n: ((n[0] + 6 - r) % 4, 0, 0, 0)),
                pl.BlockSpec((4, 1, 256, 512), lambda r, n: ((n[0] + 6 - r) % 4, 1, 0, 0)),
            ],
            out_specs=[whole, whole],
            scratch_shapes=[pltpu.VMEM((tokens, feats), F32)] * 2,
        ),
        out_shape=[jax.ShapeDtypeStruct((tokens, feats), BF16)] * 2,
        cost_estimate=cost(2 * tokens * 4096 * 512, 12 << 20),
        compiler_params=pltpu.CompilerParams(vmem_limit_bytes=12 << 20),
        name="finish",
    )(n, x, hidden, dout, gain[None], rstd, stat, weights, weights)


def pack_kernel(dest, n_ref, d, ctx, wk, wv, o0, o1, o2, o3):
    rows = wk.shape[1]
    for i, out in enumerate((o0, o1, o2, o3)):

        def share(j, carry, i=i, out=out):
            to = dest[4 * i + j]
            block = lax.rem(to // 4 + 4 - n_ref[0], 4)
            first = pl.multiple_of(lax.rem(to, 4) * 256, 256)
            part = dot(d[block, :, pl.ds(first, 256)], ctx[...], TN)
            out[j, 0:256] = part.astype(BF16)
            out[j, 256 : 256 + rows] = wk[to]
            out[j, 320 : 320 + rows] = wv[to]
            return carry

        lax.fori_loop(0, 4, share, 0)


def pack(dest, n, dout, ctx, wk, wv):
    share = jax.ShapeDtypeStruct((4, 384, ctx.shape[1]), BF16)
    return pl.pallas_call(
        pack_kernel,
        in_specs=[SMEM, SMEM, VMEM, VMEM, VMEM, VMEM],
        out_specs=[VMEM] * 4,
        out_shape=[share] * 4,
        cost_estimate=cost(ctx.shape[0] * 4096 * 512, 16 << 20),
        compiler_params=pltpu.CompilerParams(vmem_limit_bytes=16 << 20),
        name="pack",
    )(dest, n, dout, ctx, wk, wv)


def along(share, by, first):
    pairs = []
    for i in range(16):
        for core in range(2):
            x, z = i // 4, i % 4
            if (core == 0) == first:
                x = (x + by) % 4
            else:
                z = (z + by) % 4
            pairs.append((2 * i + core, 2 * (4 * x + z) + core))
    return lax.ppermute(share, ("seq", "batch"), pairs)


def first_phase(shares):
    return [shares[0]] + [along(shares[i], i, True) for i in (2, 1, 3)]


def second_phase(near):
    return [near[0]] + [along(near[j], j, False) for j in (2, 1, 3)]


def slot_tables(slot_span, n):
    slots = slot_span.shape[0]
    ids = jnp.arange(slots, dtype=jnp.int32)
    before = ids[None, :] < ids[:, None]
    same = slot_span[None, :] == slot_span[:, None]
    rank = jnp.sum(same & before, axis=1, dtype=jnp.int32)
    where = jnp.where(slot_span >= 0, slot_span * KMAX + rank, -1).astype(jnp.int32)
    spot = jnp.arange(2 * KMAX, dtype=jnp.int32)
    hit = where[None, :] == spot[:, None]
    relative = (ids + slots - 6 * n) % slots
    source = jnp.sum(jnp.where(hit, relative[None, :] + 1, 0), axis=1, dtype=jnp.int32) - 1
    counts = jnp.sum(slot_span[None, :] == jnp.arange(2)[:, None], axis=1, dtype=jnp.int32)
    return jnp.concatenate([source, counts]), where


def body(hidden, d_out, nbr_emb, slot_span, dec_gain, enc_gain, w_cond, w_enc, w_q, w_k, w_v, w_o):
    n = lax.axis_index("nbr")
    b = lax.axis_index("batch")
    n1 = n.astype(jnp.int32).reshape(1)
    tokens, feats = hidden.shape
    spans = tokens // CLEN

    kv_half = jnp.where(b == 0, w_k, w_v)
    swap = [
        ((4 * i + j) * 4 + k, ((2 * i + 2 - k) % 4 * 4 + j) * 4 + i)
        for i in range(4)
        for j in range(4)
        for k in range(4)
    ]
    qo_half = lax.ppermute(jnp.where(b == 0, w_q, w_o.T), ("seq", "nbr"), swap)
    weights = lax.all_gather(
        jnp.concatenate([qo_half, kv_half], axis=0), ("seq", "batch"), axis=0
    )

    hf = hidden.astype(F32)
    pooled = jnp.mean(hf.reshape(spans, CLEN, feats), axis=1).astype(BF16)
    squares = jnp.sum(hf * hf, axis=-1)
    length = lax.axis_size("seq")
    carried = lax.ppermute(
        pooled[spans - 1 :], "seq", [(i, i + 1) for i in range(length - 1)]
    )
    previous = jnp.concatenate([carried, pooled[: spans - 1]], axis=0)
    width = nbr_emb.shape[2]
    small = jnp.concatenate(
        [
            jnp.dot(previous, w_cond, preferred_element_type=F32),
            jnp.pad(squares, (0, width - tokens))[None],
        ],
        axis=0,
    )
    small = sum_small(small)
    condition = small[:spans]
    rstd = lax.rsqrt(small[spans, :tokens] / (4 * feats) + 1e-06)[:, None]
    normed = (hf * rstd * dec_gain.astype(F32)).astype(BF16)

    nbr_emb = lax.optimization_barrier((nbr_emb, condition))[0]
    e1, e2a, e2b, e3 = ring_gather(nbr_emb)

    tab, inv = slot_tables(slot_span, n)
    rel_span = jnp.roll(slot_span.reshape(4, 6), -n, axis=0).reshape(-1)

    def encode(block, own):
        own = own[:, None, None]
        cond = jnp.where(own == 0, condition[0], jnp.where(own == 1, condition[1], 0.0))
        x = block.astype(F32) + cond
        enc_normed = (x * rms_scale(x) * enc_gain.astype(F32)).astype(BF16)
        width = x.shape[2]
        mixed = jnp.dot(
            enc_normed.reshape(-1, width), w_enc, preferred_element_type=F32
        ).reshape(x.shape)
        return (x + jax.nn.silu(mixed)).astype(BF16)


    pairs = weights.reshape(16, 2, 312, 512)
    weights = pltpu.with_memory_space_constraint(pairs, pltpu.HBM)
    wk = pairs[:, 0, 256:].reshape(-1, 512)
    wv = pairs[:, 1, 256:].reshape(-1, 512)

    shares = project(n1, normed, d_out, weights)
    both = total(scattered(shares)).astype(BF16)
    later = lax.optimization_barrier((d_out, both))[0]
    d2, d1, d3 = (shift(later, r) for r in (2, -1, 1))
    query, d_ctx = both[:tokens], both[tokens:]
    near = jnp.concatenate([e1, e3], axis=0)
    far = jnp.concatenate([e2a, e2b], axis=0)
    encoded = [
        encode(nbr_emb, rel_span[:6]),
        encode(near, jnp.concatenate([rel_span[6:12], rel_span[18:]])),
        encode(far, rel_span[12:18]),
    ]
    enc, keys, values = keys_values(tab, encoded, wk, wv)
    ctx, d_query, d_key, d_value, parts = attend(
        tab, inv, keys, values, query, d_ctx, wk, wv
    )
    parts, d1, d2, d3 = lax.optimization_barrier((parts, d1, d2, d3))
    dout_rel = jnp.stack([d_out, d1, d2, d3])
    d_enc = lax.psum_scatter(parts, "nbr", scatter_dimension=0, tiled=True)

    place = lax.axis_index("seq")
    step = jnp.arange(4, dtype=jnp.int32)
    one, two = step[:, None], step[None, :]
    by_x, by_z = jnp.where(b == 0, one, two), jnp.where(b == 0, two, one)
    dest = (place // 4 + by_x) % 4 * 4 + (place % 4 + by_z) % 4
    dest = dest.astype(jnp.int32).reshape(-1)
    rows = enc.reshape(-1, enc.shape[2])
    wk_parts = dot(rows, d_key, TN).astype(BF16).reshape(16, -1, 512)
    wv_parts = dot(rows, d_value, TN).astype(BF16).reshape(16, -1, 512)
    arrived = first_phase(pack(dest, n1, dout_rel, ctx, wk_parts, wv_parts))
    near = [total([share[j] for share in arrived]).astype(BF16) for j in range(4)]
    last = second_phase(near)

    inner = jnp.sum(d_query.astype(F32) * query.astype(F32), axis=-1).astype(BF16)
    more = jnp.broadcast_to(jnp.pad(inner, (0, ctx.shape[1] - tokens))[None], (16, ctx.shape[1]))
    local = jnp.concatenate([ctx, d_query, more], axis=0)
    h1, h2a, h2b, h3 = ring_gather(local)
    heads = jnp.stack([local, h1, jnp.concatenate([h2a, h2b], axis=0), h3])
    heads = lax.optimization_barrier((heads, near))[0]
    stat = jnp.sum(heads[:, 2 * tokens, :tokens].astype(F32), axis=0)[:, None]
    stat = stat / (rstd * (4 * feats))
    out, d_hidden = finish(n1, heads, hidden, d_out, dec_gain, rstd, stat, weights)

    whole = total(lax.optimization_barrier((last, out))[0])
    d_wo = whole[:256].T
    d_wk, d_wv = whole[256:312], whole[320:376]
    return (out, d_hidden, d_enc, d_wo, d_wk, d_wv)


def solution(mesh):
    placed = (
        P(("batch", "seq"), "nbr"),
        P(("batch", "seq"), "nbr"),
        P(("batch", "seq", "nbr"), None, None),
        P(("batch", "seq")),
        P("nbr"),
        P(),
        P("nbr", None),
        P(),
        P("seq", "nbr"),
        P("seq", "nbr"),
        P("seq", "nbr"),
        P("nbr", "seq"),
    )
    return jax.shard_map(
        body,
        mesh=mesh,
        in_specs=placed,
        out_specs=(
            P(("batch", "seq"), "nbr"),
            P(("batch", "seq"), "nbr"),
            P(("batch", "seq", "nbr"), None, None),
            P(("batch", "nbr"), "seq"),
            P(("batch", "seq"), "nbr"),
            P(("batch", "seq"), "nbr"),
        ),
        check_vma=False,
    )
```
